256 devices in a mesh: ctx: 128 (over z, x, y), rep: 2 (over core).
Axes of the slice: x: 4, y: 4, z: 8, core: 2. Of those that a mesh axis runs over, the one named last changes fastest.
Arguments:
- queries: bfloat16 [32768, 2048], P(('rep', 'ctx')), parts along dimension 0, may hold values from -32 to 32
- encoded_key_heads: bfloat16 [32768, 256], P(('rep', 'ctx')), parts along dimension 0, may hold values from -6 to 6
- value_head_vectors: bfloat16 [32768, 256], P(('rep', 'ctx')), parts along dimension 0, may hold values from -6 to 6
- residual: bfloat16 [32768, 2048], P(('rep', 'ctx')), parts along dimension 0, may hold values from -3 to 3
- out_matrix: bfloat16 [2048, 2048], P('ctx'), may hold values from -0.125 to 0.125
- norm_gain: float32 [2048], replicated, may hold values from 0.5 to 1.5
- expert_ids: int32 [32768, 8], P(('rep', 'ctx')), parts along dimension 0, may hold values from 0 to 127, all different within a row; in each aligned block of 128 rows (0 to 127, 128 to 255, ...) at most 9 rows name the same one
- expert_gates: float32 [32768, 8], P(('rep', 'ctx')), parts along dimension 0, may hold values from 0.02 to 0.5
- gate_matrix: bfloat16 [128, 2048, 768], P('ctx'), may hold values from -0.125 to 0.125
- lift_matrix: bfloat16 [128, 2048, 768], P('ctx'), may hold values from -0.125 to 0.125
- down_matrix: bfloat16 [128, 768, 2048], P('ctx'), may hold values from -0.21875 to 0.21875
- block_mask: int32 [64, 32], P('rep'), parts along dimension 0, may hold values from 0 to 1, as said below
Outputs:
- layer_out: bfloat16 [32768, 2048], P(('rep', 'ctx')), parts along dimension 0
The draws below stay inside these ranges and needn't reach their ends.
There are 2 independent parts, one for each index of `rep`. The reference program is written for one: setup_inputs(seed, part) draws one part's arguments, and reference() takes and returns one part's arrays. A program takes and returns all parts, laid end to end along the dimension named above; an argument that names none is the same for every part. Nothing has to cross between parts.
Inputs may be any that keep to these rules, and one draw needn't show every extreme that they name: block_mask[i, j] is 1 exactly when blocks i and j belong to the same document and j <= i; a document is a run of 1 to 4 blocks, and one document has 4 blocks. `expert_ids`: each token names 8 different experts. Among the 128 tokens of one index of ctx no expert is named more than 9 times, a bound that some block reaches.
All inputs are finite; a program needn't handle non-finite values.
Results may differ from the reference program's by a relative error of at most 0.015.
Values may be sent and summed in bfloat16 or wider, within the bound.
A program may use at most 128 MiB of HBM per device.

```python
import math
from functools import partial
import jax
import jax.numpy as jnp
import numpy as np
from jax import lax

D = 2048
QUERY_HEADS = 16
KEY_VALUE_HEADS = 2
HEAD_SIZE = 128
FF = 768
TOP = 8
MASK_BLOCK_SIZE = 512
DOCUMENT_BLOCKS = 4
TOK_DEV = 128
WINDOW_TOKENS = 16384
EXPERTS = 128
CS = 9
N_CTX = 128


def query_key_pair(key):
    base = jax.random.fold_in(key, 17)
    query_seed, key_random_seed = jax.random.split(base, 2)
    query_draw = jnp.clip(jax.random.normal(query_seed, (WINDOW_TOKENS, QUERY_HEADS * HEAD_SIZE), jnp.float32), -6.0, 6.0)
    key_sample = jnp.clip(jax.random.normal(key_random_seed, (WINDOW_TOKENS, KEY_VALUE_HEADS * HEAD_SIZE), jnp.float32), -6.0, 6.0)
    return (query_draw, key_sample)


def draw_queries(key, part):
    return query_key_pair(key)[0].astype(jnp.bfloat16)


def draw_encoded_key_heads(key, part):
    return query_key_pair(key)[1].astype(jnp.bfloat16)


def draw_block_mask(key, part):
    base = jax.random.fold_in(key, 29)
    first_seed, coin_seed = jax.random.split(base, 2)
    block_count = WINDOW_TOKENS // MASK_BLOCK_SIZE
    forced = jax.random.randint(first_seed, (), 0, block_count - DOCUMENT_BLOCKS + 1)
    coin_flip = jax.random.randint(coin_seed, (block_count,), 0, 3)

    def advance(current, inputs):
        block, flip = inputs
        forced_start = (block == forced) | (block == forced + DOCUMENT_BLOCKS) | (block == 0)
        inside = (block > forced) & (block < forced + DOCUMENT_BLOCKS)
        started = forced_start | ~inside & ((current >= DOCUMENT_BLOCKS) | (flip == 0))
        current = jnp.where(started, 1, current + 1).astype(jnp.int32)
        return (current, started.astype(jnp.int32))
    _, starts = lax.scan(advance, jnp.int32(0), (jnp.arange(block_count, dtype=jnp.int32), coin_flip))
    document = jnp.cumsum(starts)
    blocks = jnp.arange(block_count, dtype=jnp.int32)
    mask = (document[:, None] == document[None, :]) & (blocks[None, :] <= blocks[:, None])
    return mask.astype(jnp.int32)


def level_of(own_key, extent, shards, low, high):
    def one(dim, shards_of):
        draws = jax.random.uniform(jax.random.fold_in(jax.random.fold_in(own_key, 6), dim), (shards_of,), jnp.float32, low / len(shards), high / len(shards))
        return jnp.repeat(jnp.exp(draws), extent[dim] // shards_of).reshape((-1,) + (1,) * (len(extent) - dim - 1))

    level = one(*shards[0])
    for cut in shards[1:]:
        level = level * one(*cut)
    return level


def shared_out(key, own, number, rows, number_of, top, bound, lean):
    ranking = jax.random.permutation(key, number_of)
    crowded, usual = portions_of(number_of, rows * top, bound, lean, True), portions_of(number_of, rows * top, bound, lean, False)
    places = jnp.arange(number_of)

    def named(lengths, turn):
        used = int((lengths > 0).sum())
        fixed = max(1, used // 4)
        moved = fixed + (places - fixed + turn * (used - fixed)) % max(1, number_of - fixed)
        return jnp.zeros((number_of,), jnp.int32).at[ranking[jnp.where(places < fixed, places, moved)]].set(jnp.asarray(lengths, jnp.int32))

    lengths = jnp.where(number % 4 == 0, named(crowded, number // 4), named(usual, number - number // 4 - 1))
    mixed = jax.random.permutation(jax.random.fold_in(own, 3), number_of)
    giver, sink = mixed[0:number_of // 2 * 2:2], mixed[1:number_of // 2 * 2:2]
    margin = jnp.minimum(lengths[giver] - 1, bound - lengths[sink]) // 2
    margin = jnp.where((giver == ranking[0]) | (sink == ranking[0]) | (lengths[sink] == 0), 0, jnp.maximum(margin, 0))
    moved = jax.random.randint(jax.random.fold_in(own, 4), (number_of // 2,), 0, 1 << 20) % (margin + 1)
    lengths = lengths.at[giver].add(-moved).at[sink].add(moved)
    labels = jnp.searchsorted(jnp.cumsum(lengths), jnp.arange(rows * top), side="right").astype(jnp.int32)
    table = labels.reshape(top, rows).T
    table = table[jax.random.permutation(jax.random.fold_in(own, 1), rows)]
    turn = jax.random.randint(jax.random.fold_in(own, 2), (rows, 1), 0, top)
    return jnp.take_along_axis(table, (jnp.arange(top)[None, :] + turn) % top, axis=1)


def portions_of(count, total, bound, lean, full):
    loads = [(1 << 20) // math.isqrt(grade ** lean) + 1 for grade in range(1, count + 1)]
    largest = bound if full else min(bound, max(-(-total // count), total * loads[0] // sum(loads)))
    least = 1 if total - largest >= count - 1 else 0
    holding, spare = [largest] + [least] * (count - 1), total - largest - least * (count - 1)
    while spare > 0:
        movable = [i for i in range(1, count) if holding[i] < largest] or [i for i in range(1, count) if holding[i] < bound]
        mass, budget = sum([loads[i] for i in movable]), spare
        for i in movable:
            addition = min(bound - holding[i], max(1, budget * loads[i] // mass), spare)
            holding[i] = holding[i] + addition
            spare = spare - addition
    return np.array(holding)


def noise(rng, extent, scale, bound, cuts=(), held_as=jnp.bfloat16):
    values = jax.random.normal(rng, extent, jnp.float32) * scale
    if len(cuts) > 0:
        values = level_of(rng, extent, cuts, -0.22, 0.18) * values
    return jnp.clip(values, min=-bound, max=bound).astype(held_as)


def setup_inputs(seed: int = 0, part: int = 0) -> dict:
    arg_keys = jax.random.split(jax.random.key(seed), 13)
    part_splits = jax.random.split(jax.random.fold_in(arg_keys[12], part), 13)
    queries = draw_queries(jax.random.fold_in(jax.random.fold_in(arg_keys[12], part), 71), part)
    encoded_key_heads = draw_encoded_key_heads(jax.random.fold_in(jax.random.fold_in(arg_keys[12], part), 71), part)
    value_head_vectors = noise(part_splits[2], (WINDOW_TOKENS, KEY_VALUE_HEADS * HEAD_SIZE), 1.0, 6.0, ((0, 128),))
    residual = noise(part_splits[3], (WINDOW_TOKENS, D), 0.5, 3.0, ((0, 128),))
    out_matrix = noise(arg_keys[4], (QUERY_HEADS * HEAD_SIZE, D), (QUERY_HEADS * HEAD_SIZE) ** -0.5, 0.125, ((0, 128),))
    norm_gain = jnp.clip(1.0 + 0.1 * jax.random.normal(arg_keys[5], (D,), jnp.float32), 0.5, 1.5)
    expert_ids_keys = jax.random.split(jax.random.fold_in(part_splits[6], 1), WINDOW_TOKENS // TOK_DEV)
    expert_ids_turns = jax.random.permutation(jax.random.fold_in(part_splits[6], 3), WINDOW_TOKENS // TOK_DEV)
    expert_ids = jax.vmap(lambda own, number: shared_out(jax.random.fold_in(part_splits[6], 2), own, number, TOK_DEV, EXPERTS, TOP, CS, 2))(expert_ids_keys, expert_ids_turns).reshape((WINDOW_TOKENS, TOP))
    expert_gates = jnp.clip(jnp.exp(math.log(0.5) - 3.218876 * jax.random.uniform(part_splits[7], (WINDOW_TOKENS, TOP), jnp.float32) ** level_of(part_splits[7], (WINDOW_TOKENS, TOP), ((0, 128),), -0.2, 0.2)), 0.02, 0.5)
    gate_matrix = noise(arg_keys[8], (EXPERTS, D, FF), D ** -0.5, 0.125, ((0, 128),))
    lift_matrix = noise(arg_keys[9], (EXPERTS, D, FF), D ** -0.5, 0.125, ((0, 128),))
    down_matrix = noise(arg_keys[10], (EXPERTS, FF, D), FF ** -0.5, 0.21875, ((0, 128),))
    block_mask = draw_block_mask(jax.random.fold_in(jax.random.fold_in(arg_keys[12], part), 71), part)
    return {"queries": queries, "encoded_key_heads": encoded_key_heads, "value_head_vectors": value_head_vectors, "residual": residual, "out_matrix": out_matrix, "norm_gain": norm_gain, "expert_ids": expert_ids, "expert_gates": expert_gates, "gate_matrix": gate_matrix, "lift_matrix": lift_matrix, "down_matrix": down_matrix, "block_mask": block_mask}


def attend_block(block_index, queries, key_padded, value_padded, block_mask):
    group_total = QUERY_HEADS // KEY_VALUE_HEADS
    first_row = block_index * MASK_BLOCK_SIZE
    query_row_block = lax.dynamic_slice_in_dim(queries, first_row, MASK_BLOCK_SIZE, 0).astype(jnp.float32)
    key_row_block = lax.dynamic_slice_in_dim(key_padded, first_row, DOCUMENT_BLOCKS * MASK_BLOCK_SIZE, 0).astype(jnp.float32)
    value_row_block = lax.dynamic_slice_in_dim(value_padded, first_row, DOCUMENT_BLOCKS * MASK_BLOCK_SIZE, 0).astype(jnp.float32)
    query_row_block = query_row_block.reshape(MASK_BLOCK_SIZE, KEY_VALUE_HEADS, group_total, HEAD_SIZE)
    key_row_block = key_row_block.reshape(DOCUMENT_BLOCKS * MASK_BLOCK_SIZE, KEY_VALUE_HEADS, HEAD_SIZE)
    value_row_block = value_row_block.reshape(DOCUMENT_BLOCKS * MASK_BLOCK_SIZE, KEY_VALUE_HEADS, HEAD_SIZE)
    scores = jnp.einsum('tagd,kad->agtk', query_row_block, key_row_block) / math.sqrt(HEAD_SIZE)
    query_place = first_row + jnp.arange(MASK_BLOCK_SIZE, dtype=jnp.int32)
    key_place = first_row - (DOCUMENT_BLOCKS - 1) * MASK_BLOCK_SIZE + jnp.arange(DOCUMENT_BLOCKS * MASK_BLOCK_SIZE, dtype=jnp.int32)
    key_block = jnp.maximum(key_place, 0) // MASK_BLOCK_SIZE
    mask_row = lax.dynamic_index_in_dim(block_mask, block_index, 0, keepdims=False)
    allowed = (key_place >= 0) & (jnp.take(mask_row, key_block) == 1)
    visible = allowed[None, :] & (key_place[None, :] <= query_place[:, None])
    scores = jnp.where(visible[None, None], scores, -jnp.inf)
    peak = lax.optimization_barrier(jnp.max(scores, axis=-1, keepdims=True))
    weights = jnp.exp(scores - peak)
    probabilities = (weights / lax.optimization_barrier(jnp.sum(weights, axis=-1, keepdims=True))).astype(jnp.bfloat16)
    blended = jnp.einsum('agtk,kad->tagd', probabilities.astype(jnp.float32), value_row_block)
    return blended.reshape(MASK_BLOCK_SIZE, QUERY_HEADS * HEAD_SIZE).astype(jnp.bfloat16)

def reference(queries, encoded_key_heads, value_head_vectors, residual, out_matrix, norm_gain, expert_ids, expert_gates, gate_matrix, lift_matrix, down_matrix, block_mask):
    pad_amount = jnp.zeros(((DOCUMENT_BLOCKS - 1) * MASK_BLOCK_SIZE, KEY_VALUE_HEADS * HEAD_SIZE), encoded_key_heads.dtype)
    key_padded = jnp.concatenate([pad_amount, encoded_key_heads], axis=0)
    value_padded = jnp.concatenate([pad_amount, value_head_vectors], axis=0)
    runner = partial(attend_block, queries=queries, key_padded=key_padded, value_padded=value_padded, block_mask=block_mask)
    attended = lax.map(runner, jnp.arange(WINDOW_TOKENS // MASK_BLOCK_SIZE, dtype=jnp.int32)).reshape(WINDOW_TOKENS, QUERY_HEADS * HEAD_SIZE)
    projected = jnp.dot(attended, out_matrix, preferred_element_type=jnp.float32)
    hidden_state = (residual.astype(jnp.float32) + projected).astype(jnp.bfloat16)
    widened = hidden_state.astype(jnp.float32)
    normed = (widened * lax.rsqrt(lax.optimization_barrier(jnp.mean(widened * widened, axis=-1, keepdims=True)) + 1e-06) * norm_gain.astype(jnp.float32)).astype(jnp.bfloat16)
    capacity = N_CTX * CS

    def expert_step(combined, inputs):
        gate_slab, lift_slab, down_slab, expert = inputs
        chosen = expert_ids == expert
        weight = lax.optimization_barrier(jnp.sum(jnp.where(chosen, expert_gates, 0.0), axis=1))
        picked = jnp.any(chosen, axis=1)
        row_index = jnp.nonzero(picked, size=capacity, fill_value=0)[0].astype(jnp.int32)
        filled = jnp.arange(capacity, dtype=jnp.int32) < jnp.sum(picked.astype(jnp.int32))
        gathered = normed[row_index]
        gate_act = jnp.dot(gathered, gate_slab, preferred_element_type=jnp.float32)
        lift_act = jnp.dot(gathered, lift_slab, preferred_element_type=jnp.float32)
        activated = (jax.nn.silu(gate_act) * lift_act).astype(jnp.bfloat16)
        produced = jnp.dot(activated, down_slab, preferred_element_type=jnp.float32).astype(jnp.bfloat16)
        factor_rows = jnp.where(filled, weight[row_index], 0.0)
        combined = combined.at[row_index].add(factor_rows[:, None] * produced.astype(jnp.float32))
        return (combined, None)
    expert_sum, _ = lax.scan(expert_step, jnp.zeros((WINDOW_TOKENS, D), jnp.float32), (gate_matrix, lift_matrix, down_matrix, jnp.arange(EXPERTS, dtype=jnp.int32)))
    return (widened + expert_sum).astype(jnp.bfloat16)
```

```python
import math

import jax
import jax.numpy as jnp
from jax import lax
from jax.experimental import pallas as pl
from jax.experimental.pallas import tpu as pltpu
from jax.sharding import PartitionSpec as P

QUERY_HEADS = 16
KEY_VALUE_HEADS = 2
HEAD_SIZE = 128
TOP = 8
MASK_BLOCK_SIZE = 512
DOCUMENT_BLOCKS = 4


MESH_ID = pl.DeviceIdType.MESH
PLANE = ((1, 0), (3, 0), (0, 1), (0, 3), (1, 1), (3, 3), (1, 3), (3, 1), (2, 0), (0, 2), (2, 1), (2, 3), (1, 2), (3, 2), (2, 2))
CAP = 9
NX, NY, NZ = 4, 4, 8
NQ = NX * NY


def moe_kernel(
    x_ref,
    h_ref,
    m_ref,
    wg_hbm,
    wl_hbm,
    wd_hbm,
    o_ref,
    wg,
    wl,
    wd,
    xg,
    meta,
    keys,
    gts,
    outbox,
    inbox,
    ret,
    xs,
    act,
    part,
    rsend,
    rrecv,
    w_sem,
    zs,
    zr,
    ms,
    mr,
    ds_,
    dr,
    bs,
    br,
    ss,
    sr,
):
    f32, bf16 = jnp.float32, jnp.bfloat16
    width = x_ref.shape[1]
    half = x_ref.shape[0] // 2
    me = lax.axis_index("ctx")
    z = me // NQ
    q = lax.rem(me, NQ)
    qx, qy = q // NY, lax.rem(q, NY)

    def zpeer(d):
        return lax.rem(z + d, NZ) * NQ + q

    def qpeer(i):
        return lax.rem(qx + PLANE[i][0], NX) * NY + lax.rem(qy + PLANE[i][1], NY)

    def remote(src, dst, s_sem, r_sem, dev):
        return pltpu.make_async_remote_copy(
            src_ref=src, dst_ref=dst, send_sem=s_sem, recv_sem=r_sem, device_id={"ctx": dev}, device_id_type=MESH_ID
        )

    weights = [
        pltpu.make_async_copy(a, b, w_sem.at[i])
        for i, (a, b) in enumerate(((wg_hbm.at[0], wg), (wl_hbm.at[0], wl), (wd_hbm.at[0], wd)))
    ]
    for c in weights:
        c.start()

    barrier = pltpu.get_barrier_semaphore()
    for d in range(1, NZ):
        pl.semaphore_signal(barrier, inc=1, device_id={"ctx": zpeer(d)}, device_id_type=MESH_ID)
    for i in range(NQ - 1):
        pl.semaphore_signal(barrier, inc=1, device_id={"ctx": z * NQ + qpeer(i)}, device_id_type=MESH_ID)
    pl.semaphore_wait(barrier, NZ - 1 + NQ - 1)

    slot_of = {0: 0, 1: 1, 7: 2, 2: 3, 6: 4, 3: 5, 5: 6, 4: 7}

    def zcopy(d, k, h):
        src = x_ref if k == 0 else xg.at[2 * k - 1 + d]
        rows = pl.ds(h * half, half)
        dst = xg.at[2 * k + 1 + d] if k < 3 else xg.at[7]
        return remote(src.at[rows], dst.at[rows], zs.at[d, k, h], zr.at[d, k, h], zpeer(1 if d == 0 else NZ - 1))

    def zparts(k):
        return [(d, h) for h in range(2) for d in range(2) if k < 3 or d == h]

    for d, h in zparts(0):
        zcopy(d, 0, h).start()
    mcopies = []
    for d in range(1, NZ):
        mcopies.append(remote(m_ref, meta.at[slot_of[d]], ms.at[d - 1], mr.at[d - 1], zpeer(d)))
    for c in mcopies:
        c.start()
    meta[0] = m_ref[...]
    xg[0] = x_ref[...]

    tokens = m_ref.shape[1]
    tri = (
        lax.broadcasted_iota(jnp.int32, (tokens, tokens), 0) < lax.broadcasted_iota(jnp.int32, (tokens, tokens), 1)
    ).astype(bf16)
    expert = (lax.broadcasted_iota(jnp.int32, (NQ, tokens), 0) + z * NQ).astype(f32)

    def block_keys(b):
        rows = meta[b]
        chosen = jnp.zeros((NQ, tokens), f32)
        gate = jnp.zeros((NQ, tokens), f32)
        for k in range(TOP):
            hit = expert == rows[k : k + 1, :]
            chosen = jnp.where(hit, 1.0, chosen)
            gate = jnp.where(hit, rows[TOP + k : TOP + k + 1, :], gate)
        rank = jnp.dot(chosen.astype(bf16), tri, preferred_element_type=f32)
        keys[b] = jnp.where(chosen > 0.5, rank, -100.0)
        gts[b] = gate

    row = lax.broadcasted_iota(jnp.int32, (NQ, 8, tokens), 1)

    def hits(b, first):
        return keys[b][:, None, :] == (row + first).astype(f32)

    def pick(b, first):
        return jnp.where(hits(b, first), 1.0, 0.0).reshape(NQ * 8, tokens).astype(bf16)

    def build(t, blocks):
        mats = [pick(b, first) for b, first in blocks]
        chunk = width // 4

        def piece(c, carry):
            cols = pl.ds(pl.multiple_of(c * chunk, chunk), chunk)
            total = None
            for (b, _), mat in zip(blocks, mats):
                one = jnp.dot(mat, xg[b, :, cols], preferred_element_type=f32)
                total = one if total is None else total + one
            outbox[t, :, :, cols] = total.astype(bf16).reshape(NQ, 8, chunk)
            return carry

        lax.fori_loop(0, 4, piece, 0)
        for i in range(NQ - 1):
            p = qpeer(i)
            remote(outbox.at[t, p], inbox.at[t, q], ds_.at[t], dr.at[t], z * NQ + p).start()
        inbox[t, q] = outbox[t, q]

    def dispatch(t):
        if isinstance(t, int) and t == 0:
            build(0, [(0, 0)])
        elif isinstance(t, int) and t == 8:
            build(8, [(7, 1)])
        else:
            build(t, [(t - 1, 9 - t), (t, -t)])

    def wait_all(buf, sem):
        pltpu.make_async_copy(buf, buf, sem).wait()

    def mlp(first, count):
        rows = count * NQ * 8

        def take(t, carry):
            wait_all(inbox.at[first + t, pl.ds(0, NQ - 1)], dr.at[first + t])
            xs[pl.ds(pl.multiple_of(t * NQ * 8, NQ * 8), NQ * 8), :] = inbox[first + t].reshape(NQ * 8, width)
            return carry

        lax.fori_loop(0, count, take, 0)
        hidden = wg.shape[1]
        tile = 256

        def up(c, carry):
            cols = pl.ds(pl.multiple_of(c * tile, tile), tile)
            g = jnp.dot(xs[pl.ds(0, rows), :], wg[:, cols], preferred_element_type=f32)
            u = jnp.dot(xs[pl.ds(0, rows), :], wl[:, cols], preferred_element_type=f32)
            act[pl.ds(0, rows), cols] = (g / (1.0 + jnp.exp(-g)) * u).astype(bf16)
            return carry

        lax.fori_loop(0, hidden // tile, up, 0)

        def down(c, carry):
            cols = pl.ds(pl.multiple_of(c * tile, tile), tile)
            y = jnp.dot(act[pl.ds(0, rows), :], wd[:, cols], preferred_element_type=f32)
            inbox[pl.ds(first, count), :, :, cols] = y.astype(bf16).reshape(count, NQ, 8, tile)
            return carry

        lax.fori_loop(0, width // tile, down, 0)

    def give_back(t):
        for i in range(NQ - 1):
            p = qpeer(i)
            remote(inbox.at[t, p], ret.at[t, q], bs.at[t], br.at[t], z * NQ + p).start()
        ret[t, q] = inbox[t, q]

    block_keys(0)
    dispatch(0)
    for c in mcopies:
        c.wait()

    def more_keys(b, carry):
        block_keys(b)
        return carry

    lax.fori_loop(1, NZ, more_keys, 0)
    groups = ((0, 3), (3, 2), (5, 2), (7, 2))
    for k in range(4):
        for d, h in zparts(k):
            zcopy(d, k, h).wait_recv()
            if k < 3 and (d, h) in zparts(k + 1):
                zcopy(d, k + 1, h).start()
        if k < 3:

            def two(t, carry):
                dispatch(t)
                return carry

            lax.fori_loop(2 * k + 1, 2 * k + 3, two, 0)
        else:
            dispatch(7)
            dispatch(8)
        if k == 0:
            for c in weights:
                c.wait()
        else:
            mlp(*groups[k - 1])
    mlp(*groups[3])

    def back(t, carry):
        give_back(8 - t)
        return carry

    lax.fori_loop(0, 9, back, 0)

    def wait_ret(t):
        wait_all(ret.at[t, pl.ds(0, NQ - 1)], br.at[t])

    def partial(b, slot):
        lo = jnp.where(hits(b, -b), gts[b][:, None, :], 0.0).reshape(NQ * 8, tokens)
        hi = jnp.where(hits(b, 8 - b), gts[b][:, None, :], 0.0).reshape(NQ * 8, tokens)
        mat = jnp.concatenate([lo, hi], axis=0).T.astype(bf16)
        chunk = width // 4

        def piece(c, carry):
            cols = pl.ds(pl.multiple_of(c * chunk, chunk), chunk)
            rows = ret[b : b + 2, :, :, cols].reshape(2 * NQ * 8, chunk)
            part[slot, :, cols] = jnp.dot(mat, rows, preferred_element_type=f32)
            return carry

        lax.fori_loop(0, 4, piece, 0)

    def scopy(d, k, h):
        rows = pl.ds(h * half, half)
        return remote(
            rsend.at[d, k, rows], rrecv.at[d, k, rows], ss.at[d, k, h], sr.at[d, k, h], zpeer(1 if d == 0 else NZ - 1)
        )

    def sparts(k):
        return [(d, h) for h in range(2) for d in range(2) if k > 0 or d == h]

    wait_ret(8)
    wait_ret(7)
    partial(7, 0)
    for d, h in sparts(0):
        rows = pl.ds(h * half, half)
        rsend[d, 0, rows] = part[0, rows].astype(bf16)
        scopy(d, 0, h).start()
    for k in range(1, 4):
        wait_ret(8 - 2 * k)
        wait_ret(7 - 2 * k)
        partial(8 - 2 * k, 0)
        partial(7 - 2 * k, 1)
        for d, h in sparts(k):
            rows = pl.ds(h * half, half)
            total = part[d, rows]
            if (d, h) in sparts(k - 1):
                scopy(d, k - 1, h).wait_recv()
                total = total + rrecv[d, k - 1, rows].astype(f32)
            rsend[d, k, rows] = total.astype(bf16)
            scopy(d, k, h).start()
    wait_ret(0)
    partial(0, 0)
    for h in range(2):
        rows = pl.ds(h * half, half)
        total = part[0, rows] + h_ref[rows, :].astype(f32)
        for d in range(2):
            scopy(d, 3, h).wait_recv()
            total = total + rrecv[d, 3, rows].astype(f32)
        o_ref[rows, :] = total.astype(bf16)

    for k in range(4):
        for d, h in zparts(k):
            zcopy(d, k, h).wait_send()
        for d, h in sparts(k):
            scopy(d, k, h).wait_send()

    def sent(t, carry):
        wait_all(outbox.at[t, pl.ds(0, NQ - 1)], ds_.at[t])
        wait_all(inbox.at[t, pl.ds(0, NQ - 1)], bs.at[t])
        return carry

    lax.fori_loop(0, 9, sent, 0)


def moe(normed, hidden_state, meta, gate_matrix, lift_matrix, down_matrix):
    rows, width = normed.shape
    ff = gate_matrix.shape[2]
    bf16, f32 = jnp.bfloat16, jnp.float32
    vmem = pl.BlockSpec(memory_space=pltpu.VMEM)
    hbm = pl.BlockSpec(memory_space=pl.ANY)
    dma = pltpu.SemaphoreType.DMA
    return pl.pallas_call(
        moe_kernel,
        out_shape=jax.ShapeDtypeStruct((rows, width), bf16),
        in_specs=[vmem, vmem, vmem, hbm, hbm, hbm],
        out_specs=vmem,
        scratch_shapes=[
            pltpu.VMEM((width, ff), bf16),
            pltpu.VMEM((width, ff), bf16),
            pltpu.VMEM((ff, width), bf16),
            pltpu.VMEM((NZ, rows, width), bf16),
            pltpu.VMEM((NZ, 2 * TOP, rows), f32),
            pltpu.VMEM((NZ, NQ, rows), f32),
            pltpu.VMEM((NZ, NQ, rows), f32),
            pltpu.VMEM((CAP, NQ, 8, width), bf16),
            pltpu.VMEM((CAP, NQ, 8, width), bf16),
            pltpu.VMEM((CAP, NQ, 8, width), bf16),
            pltpu.VMEM((3 * NQ * 8, width), bf16),
            pltpu.VMEM((3 * NQ * 8, ff), bf16),
            pltpu.VMEM((2, rows, width), f32),
            pltpu.VMEM((2, 4, rows, width), bf16),
            pltpu.VMEM((2, 4, rows, width), bf16),
            dma((3,)),
            dma((2, 4, 2)),
            dma((2, 4, 2)),
            dma((NZ - 1,)),
            dma((NZ - 1,)),
            dma((CAP,)),
            dma((CAP,)),
            dma((CAP,)),
            dma((CAP,)),
            dma((2, 4, 2)),
            dma((2, 4, 2)),
        ],
        compiler_params=pltpu.CompilerParams(collective_id=0, has_side_effects=True, vmem_limit_bytes=60 * 1024 * 1024),
        name="moe",
    )(normed, hidden_state, meta, gate_matrix, lift_matrix, down_matrix)


def shifted(value, axis, steps):
    count = lax.axis_size(axis)
    initial, last = (max(0, -steps), min(count, count - steps))
    return lax.ppermute(value, axis, [(source, source + steps) for source in range(initial, last)])


def attend(queries, document_window, block_mask, block_extent):
    total_row_count = queries.shape[0]
    group_total = QUERY_HEADS // KEY_VALUE_HEADS
    device = lax.axis_index("ctx")
    per_block = MASK_BLOCK_SIZE // total_row_count
    query_block = device // per_block
    shard_device = device - (block_extent - 1) + jnp.arange(block_extent, dtype=jnp.int32)
    shard_block = jnp.maximum(shard_device, 0) // per_block
    mask_row = lax.dynamic_index_in_dim(block_mask, query_block, 0, keepdims=False)
    block_ids = jnp.arange(block_mask.shape[1], dtype=jnp.int32)
    lookup = jnp.sum(
        jnp.where(shard_block[:, None] == block_ids[None, :], mask_row[None, :], 0), axis=1
    )
    shard_open = (shard_device >= 0) & (lookup == 1)
    flat = jnp.arange(block_extent * total_row_count, dtype=jnp.int32)
    shard_of = flat // total_row_count
    place_of = flat % total_row_count
    open_key = jnp.take(shard_open, shard_of)
    query_place = jnp.arange(total_row_count, dtype=jnp.int32)
    visible = open_key[None, :] & (
        (shard_of[None, :] < block_extent - 1) | (place_of[None, :] <= query_place[:, None])
    )
    key_flattened = document_window[:, 0].reshape(
        block_extent * total_row_count, KEY_VALUE_HEADS, HEAD_SIZE
    )
    value_flattened = document_window[:, 1].reshape(
        block_extent * total_row_count, KEY_VALUE_HEADS, HEAD_SIZE
    )
    query_partition = queries.reshape(total_row_count, KEY_VALUE_HEADS, group_total, HEAD_SIZE)
    outputs = []
    for group_of_head in range(KEY_VALUE_HEADS):
        scores = jnp.einsum(
            "tgd,kd->gtk",
            query_partition[:, group_of_head],
            key_flattened[:, group_of_head],
            preferred_element_type=jnp.float32,
        ) / math.sqrt(HEAD_SIZE)
        scores = jnp.where(visible[None], scores, -jnp.inf)
        peak = jnp.max(scores, axis=-1, keepdims=True)
        weights = jnp.exp(scores - peak)
        probabilities = (weights / jnp.sum(weights, axis=-1, keepdims=True)).astype(jnp.bfloat16)
        blended = jnp.einsum(
            "gtk,kd->tgd",
            probabilities,
            value_flattened[:, group_of_head],
            preferred_element_type=jnp.float32,
        )
        outputs.append(blended.astype(jnp.bfloat16))
    return jnp.stack(outputs, axis=1).reshape(total_row_count, QUERY_HEADS * HEAD_SIZE)


def shards(
    queries,
    encoded_key_heads,
    value_head_vectors,
    residual,
    out_matrix,
    norm_gain,
    expert_ids,
    expert_gates,
    gate_matrix,
    lift_matrix,
    down_matrix,
    block_mask,
):
    total_row_count = queries.shape[0]
    devices = lax.axis_size("ctx")
    block_extent = DOCUMENT_BLOCKS * MASK_BLOCK_SIZE // total_row_count
    model_width = out_matrix.shape[1]
    paired = jnp.stack([encoded_key_heads, value_head_vectors])
    earlier = [shifted(paired, "ctx", distance) for distance in range(block_extent - 1, 0, -1)]
    document_window = jnp.stack(earlier + [paired])
    attended = attend(queries, document_window, block_mask, block_extent)
    projected = jnp.dot(
        attended,
        lax.all_gather(out_matrix, "ctx", axis=0, tiled=True),
        preferred_element_type=jnp.float32,
    )
    hidden_state = (residual.astype(jnp.float32) + projected).astype(jnp.bfloat16)
    widened = hidden_state.astype(jnp.float32)
    normed = (
        widened * lax.rsqrt(jnp.mean(widened * widened, axis=-1, keepdims=True) + 1e-06) * norm_gain
    ).astype(jnp.bfloat16)
    meta = jnp.concatenate([expert_ids.astype(jnp.float32).T, expert_gates.T])
    return moe(normed, hidden_state, meta, gate_matrix, lift_matrix, down_matrix)


def solution(mesh):
    placed = (
        P(("rep", "ctx"), None),
        P(("rep", "ctx"), None),
        P(("rep", "ctx"), None),
        P(("rep", "ctx"), None),
        P("ctx", None),
        P(),
        P(("rep", "ctx"), None),
        P(("rep", "ctx"), None),
        P("ctx", None, None),
        P("ctx", None, None),
        P("ctx", None, None),
        P("rep", None),
    )
    return jax.shard_map(
        shards, mesh=mesh, in_specs=placed, out_specs=P(("rep", "ctx"), None), check_vma=False
    )
```

```python
import math

import jax
import jax.numpy as jnp
from jax import lax
from jax.experimental import pallas as pl
from jax.experimental.pallas import tpu as pltpu
from jax.sharding import PartitionSpec as P

QUERY_HEADS = 16
KEY_VALUE_HEADS = 2
HEAD_SIZE = 128
TOP = 8
MASK_BLOCK_SIZE = 512
DOCUMENT_BLOCKS = 4


MESH_ID = pl.DeviceIdType.MESH
PLANE = ((1, 0), (3, 0), (0, 1), (0, 3), (1, 1), (3, 3), (1, 3), (3, 1), (2, 0), (0, 2), (2, 1), (2, 3), (1, 2), (3, 2), (2, 2))
CAP = 9
NX, NY, NZ = 4, 4, 8
NQ = NX * NY


def moe_kernel(
    x_ref,
    h_ref,
    m_ref,
    wg_hbm,
    wl_hbm,
    wd_hbm,
    o_ref,
    wg,
    wl,
    wd,
    xg,
    meta,
    keys,
    gts,
    outbox,
    inbox,
    ret,
    xs,
    act,
    part,
    rsend,
    rrecv,
    w_sem,
    zs,
    zr,
    ms,
    mr,
    ds_,
    dr,
    bs,
    br,
    ss,
    sr,
):
    f32, bf16 = jnp.float32, jnp.bfloat16
    width = x_ref.shape[1]
    half = x_ref.shape[0] // 2
    me = lax.axis_index("ctx")
    z = me // NQ
    q = lax.rem(me, NQ)
    qx, qy = q // NY, lax.rem(q, NY)

    def zpeer(d):
        return lax.rem(z + d, NZ) * NQ + q

    def qpeer(i):
        return lax.rem(qx + PLANE[i][0], NX) * NY + lax.rem(qy + PLANE[i][1], NY)

    def remote(src, dst, s_sem, r_sem, dev):
        return pltpu.make_async_remote_copy(
            src_ref=src, dst_ref=dst, send_sem=s_sem, recv_sem=r_sem, device_id={"ctx": dev}, device_id_type=MESH_ID
        )

    weights = [
        pltpu.make_async_copy(a, b, w_sem.at[i])
        for i, (a, b) in enumerate(((wg_hbm.at[0], wg), (wl_hbm.at[0], wl), (wd_hbm.at[0], wd)))
    ]
    for c in weights:
        c.start()

    barrier = pltpu.get_barrier_semaphore()
    for d in range(1, NZ):
        pl.semaphore_signal(barrier, inc=1, device_id={"ctx": zpeer(d)}, device_id_type=MESH_ID)
    for i in range(NQ - 1):
        pl.semaphore_signal(barrier, inc=1, device_id={"ctx": z * NQ + qpeer(i)}, device_id_type=MESH_ID)
    pl.semaphore_wait(barrier, NZ - 1 + NQ - 1)

    slot_of = {0: 0, 1: 1, 7: 2, 2: 3, 6: 4, 3: 5, 5: 6, 4: 7}

    def zcopy(d, k, h):
        src = x_ref if k == 0 else xg.at[2 * k - 1 + d]
        rows = pl.ds(h * half, half)
        dst = xg.at[2 * k + 1 + d] if k < 3 else xg.at[7]
        return remote(src.at[rows], dst.at[rows], zs.at[d, k, h], zr.at[d, k, h], zpeer(1 if d == 0 else NZ - 1))

    def zparts(k):
        return [(d, h) for h in range(2) for d in range(2) if k < 3 or d == h]

    for d, h in zparts(0):
        zcopy(d, 0, h).start()
    mcopies = []
    for d in range(1, NZ):
        mcopies.append(remote(m_ref, meta.at[slot_of[d]], ms.at[d - 1], mr.at[d - 1], zpeer(d)))
    for c in mcopies:
        c.start()
    meta[0] = m_ref[...]
    xg[0] = x_ref[...]

    tokens = m_ref.shape[1]
    tri = (
        lax.broadcasted_iota(jnp.int32, (tokens, tokens), 0) < lax.broadcasted_iota(jnp.int32, (tokens, tokens), 1)
    ).astype(bf16)
    expert = (lax.broadcasted_iota(jnp.int32, (NQ, tokens), 0) + z * NQ).astype(f32)

    def block_keys(b):
        rows = meta[b]
        chosen = jnp.zeros((NQ, tokens), f32)
        gate = jnp.zeros((NQ, tokens), f32)
        for k in range(TOP):
            hit = expert == rows[k : k + 1, :]
            chosen = jnp.where(hit, 1.0, chosen)
            gate = jnp.where(hit, rows[TOP + k : TOP + k + 1, :], gate)
        rank = jnp.dot(chosen.astype(bf16), tri, preferred_element_type=f32)
        keys[b] = jnp.where(chosen > 0.5, rank, -100.0)
        gts[b] = gate

    row = lax.broadcasted_iota(jnp.int32, (NQ, 8, tokens), 1)

    def hits(b, first):
        return keys[b][:, None, :] == (row + first).astype(f32)

    def pick(b, first):
        return jnp.where(hits(b, first), 1.0, 0.0).reshape(NQ * 8, tokens).astype(bf16)

    def build(t, blocks):
        mats = [pick(b, first) for b, first in blocks]
        chunk = width // 4

        def piece(c, carry):
            cols = pl.ds(pl.multiple_of(c * chunk, chunk), chunk)
            total = None
            for (b, _), mat in zip(blocks, mats):
                one = jnp.dot(mat, xg[b, :, cols], preferred_element_type=f32)
                total = one if total is None else total + one
            outbox[t, :, :, cols] = total.astype(bf16).reshape(NQ, 8, chunk)
            return carry

        lax.fori_loop(0, 4, piece, 0)
        for i in range(NQ - 1):
            p = qpeer(i)
            remote(outbox.at[t, p], inbox.at[t, q], ds_.at[t], dr.at[t], z * NQ + p).start()
        inbox[t, q] = outbox[t, q]

    def dispatch(t):
        if isinstance(t, int) and t == 0:
            build(0, [(0, 0)])
        elif isinstance(t, int) and t == 8:
            build(8, [(7, 1)])
        else:
            build(t, [(t - 1, 9 - t), (t, -t)])

    def wait_all(buf, sem):
        pltpu.make_async_copy(buf, buf, sem).wait()

    def mlp(first, count):
        rows = count * NQ * 8

        def take(t, carry):
            wait_all(inbox.at[first + t, pl.ds(0, NQ - 1)], dr.at[first + t])
            xs[pl.ds(pl.multiple_of(t * NQ * 8, NQ * 8), NQ * 8), :] = inbox[first + t].reshape(NQ * 8, width)
            return carry

        lax.fori_loop(0, count, take, 0)
        hidden = wg.shape[1]
        tile = 256

        def up(c, carry):
            cols = pl.ds(pl.multiple_of(c * tile, tile), tile)
            g = jnp.dot(xs[pl.ds(0, rows), :], wg[:, cols], preferred_element_type=f32)
            u = jnp.dot(xs[pl.ds(0, rows), :], wl[:, cols], preferred_element_type=f32)
            act[pl.ds(0, rows), cols] = (g / (1.0 + jnp.exp(-g)) * u).astype(bf16)
            return carry

        lax.fori_loop(0, hidden // tile, up, 0)

        def down(c, carry):
            cols = pl.ds(pl.multiple_of(c * tile, tile), tile)
            y = jnp.dot(act[pl.ds(0, rows), :], wd[:, cols], preferred_element_type=f32)
            inbox[pl.ds(first, count), :, :, cols] = y.astype(bf16).reshape(count, NQ, 8, tile)
            return carry

        lax.fori_loop(0, width // tile, down, 0)

    def give_back(t):
        for i in range(NQ - 1):
            p = qpeer(i)
            remote(inbox.at[t, p], ret.at[t, q], bs.at[t], br.at[t], z * NQ + p).start()
        ret[t, q] = inbox[t, q]

    block_keys(0)
    dispatch(0)
    for c in mcopies:
        c.wait()

    def more_keys(b, carry):
        block_keys(b)
        return carry

    lax.fori_loop(1, NZ, more_keys, 0)
    groups = ((0, 3), (3, 2), (5, 2), (7, 2))
    for k in range(4):
        for d, h in zparts(k):
            zcopy(d, k, h).wait_recv()
            if k < 3 and (d, h) in zparts(k + 1):
                zcopy(d, k + 1, h).start()
        if k < 3:

            def two(t, carry):
                dispatch(t)
                return carry

            lax.fori_loop(2 * k + 1, 2 * k + 3, two, 0)
        else:
            dispatch(7)
            dispatch(8)
        if k == 0:
            for c in weights:
                c.wait()
        else:
            mlp(*groups[k - 1])
    mlp(*groups[3])

    def back(t, carry):
        give_back(8 - t)
        return carry

    lax.fori_loop(0, 9, back, 0)

    def wait_ret(t):
        wait_all(ret.at[t, pl.ds(0, NQ - 1)], br.at[t])

    def partial(b, slot):
        lo = jnp.where(hits(b, -b), gts[b][:, None, :], 0.0).reshape(NQ * 8, tokens)
        hi = jnp.where(hits(b, 8 - b), gts[b][:, None, :], 0.0).reshape(NQ * 8, tokens)
        mat = jnp.concatenate([lo, hi], axis=0).T.astype(bf16)
        chunk = width // 4

        def piece(c, carry):
            cols = pl.ds(pl.multiple_of(c * chunk, chunk), chunk)
            rows = ret[b : b + 2, :, :, cols].reshape(2 * NQ * 8, chunk)
            part[slot, :, cols] = jnp.dot(mat, rows, preferred_element_type=f32)
            return carry

        lax.fori_loop(0, 4, piece, 0)

    def scopy(d, k, h):
        rows = pl.ds(h * half, half)
        return remote(
            rsend.at[d, k, rows], rrecv.at[d, k, rows], ss.at[d, k, h], sr.at[d, k, h], zpeer(1 if d == 0 else NZ - 1)
        )

    def sparts(k):
        return [(d, h) for h in range(2) for d in range(2) if k > 0 or d == h]

    wait_ret(8)
    wait_ret(7)
    partial(7, 0)
    for d, h in sparts(0):
        rows = pl.ds(h * half, half)
        rsend[d, 0, rows] = part[0, rows].astype(bf16)
        scopy(d, 0, h).start()
    for k in range(1, 4):
        wait_ret(8 - 2 * k)
        wait_ret(7 - 2 * k)
        partial(8 - 2 * k, 0)
        partial(7 - 2 * k, 1)
        for d, h in sparts(k):
            rows = pl.ds(h * half, half)
            total = part[d, rows]
            if (d, h) in sparts(k - 1):
                scopy(d, k - 1, h).wait_recv()
                total = total + rrecv[d, k - 1, rows].astype(f32)
            rsend[d, k, rows] = total.astype(bf16)
            scopy(d, k, h).start()
    wait_ret(0)
    partial(0, 0)
    for h in range(2):
        rows = pl.ds(h * half, half)
        total = part[0, rows] + h_ref[rows, :].astype(f32)
        for d in range(2):
            scopy(d, 3, h).wait_recv()
            total = total + rrecv[d, 3, rows].astype(f32)
        o_ref[rows, :] = total.astype(bf16)

    for k in range(4):
        for d, h in zparts(k):
            zcopy(d, k, h).wait_send()
        for d, h in sparts(k):
            scopy(d, k, h).wait_send()

    def sent(t, carry):
        wait_all(outbox.at[t, pl.ds(0, NQ - 1)], ds_.at[t])
        wait_all(inbox.at[t, pl.ds(0, NQ - 1)], bs.at[t])
        return carry

    lax.fori_loop(0, 9, sent, 0)


def moe(normed, hidden_state, meta, gate_matrix, lift_matrix, down_matrix):
    rows, width = normed.shape
    ff = gate_matrix.shape[2]
    bf16, f32 = jnp.bfloat16, jnp.float32
    vmem = pl.BlockSpec(memory_space=pltpu.VMEM)
    hbm = pl.BlockSpec(memory_space=pl.ANY)
    dma = pltpu.SemaphoreType.DMA
    return pl.pallas_call(
        moe_kernel,
        out_shape=jax.ShapeDtypeStruct((rows, width), bf16),
        in_specs=[vmem, vmem, vmem, hbm, hbm, hbm],
        out_specs=vmem,
        scratch_shapes=[
            pltpu.VMEM((width, ff), bf16),
            pltpu.VMEM((width, ff), bf16),
            pltpu.VMEM((ff, width), bf16),
            pltpu.VMEM((NZ, rows, width), bf16),
            pltpu.VMEM((NZ, 2 * TOP, rows), f32),
            pltpu.VMEM((NZ, NQ, rows), f32),
            pltpu.VMEM((NZ, NQ, rows), f32),
            pltpu.VMEM((CAP, NQ, 8, width), bf16),
            pltpu.VMEM((CAP, NQ, 8, width), bf16),
            pltpu.VMEM((CAP, NQ, 8, width), bf16),
            pltpu.VMEM((3 * NQ * 8, width), bf16),
            pltpu.VMEM((3 * NQ * 8, ff), bf16),
            pltpu.VMEM((2, rows, width), f32),
            pltpu.VMEM((2, 4, rows, width), bf16),
            pltpu.VMEM((2, 4, rows, width), bf16),
            dma((3,)),
            dma((2, 4, 2)),
            dma((2, 4, 2)),
            dma((NZ - 1,)),
            dma((NZ - 1,)),
            dma((CAP,)),
            dma((CAP,)),
            dma((CAP,)),
            dma((CAP,)),
            dma((2, 4, 2)),
            dma((2, 4, 2)),
        ],
        compiler_params=pltpu.CompilerParams(collective_id=0, has_side_effects=True, vmem_limit_bytes=60 * 1024 * 1024),
        name="moe",
    )(normed, hidden_state, meta, gate_matrix, lift_matrix, down_matrix)


NEG = -1e30


def attn_kernel(
    q_ref,
    k_ref,
    v_ref,
    r_ref,
    w_ref,
    g_ref,
    b_ref,
    n_ref,
    h_ref,
    kbuf,
    vbuf,
    wfull,
    bias,
    s_ref,
    p_ref,
    l_ref,
    att,
    snd,
    rcv,
):
    f32, bf16 = jnp.float32, jnp.bfloat16
    tokens, width = q_ref.shape
    me = lax.axis_index("ctx")
    r = lax.axis_index("rep")
    z = me // NQ
    x, y = lax.rem(me, NQ) // NY, lax.rem(me, NY)
    total = NQ * NZ
    used = [0]

    def at(dz, dx, dy):
        return {"ctx": lax.rem(z + dz, NZ) * NQ + lax.rem(x + dx, NX) * NY + lax.rem(y + dy, NY)}

    def later(j):
        return {"ctx": lax.rem(me + j * NY, total)}

    def send(src, dst, dev):
        i = used[0]
        used[0] += 1
        c = pltpu.make_async_remote_copy(
            src_ref=src, dst_ref=dst, send_sem=snd.at[i], recv_sem=rcv.at[i], device_id=dev, device_id_type=MESH_ID
        )
        c.start()
        copies.append(c)
        return c

    copies = []
    partner = {"rep": 1 - r}
    barrier = pltpu.get_barrier_semaphore()
    peers = [at(d, 0, 0) for d in range(1, NZ)] + [at(0, d, 0) for d in range(1, NX)] + [at(0, 0, d) for d in range(1, NY)]
    peers += [partner] + [later(j) for j in range(1, DOCUMENT_BLOCKS)]
    peers += [later(NQ * NZ // NY - j) for j in range(1, DOCUMENT_BLOCKS)]
    for dev in peers:
        pl.semaphore_signal(barrier, inc=1, device_id=dev, device_id_type=MESH_ID)
    pl.semaphore_wait(barrier, len(peers))

    def landed(cs):
        for c in cs:
            c.wait_recv()

    order = (1, 3, 2)
    half, quarter = width // 2, width // 4
    pc, pa, pb = pl.ds(0, half), pl.ds(half, quarter), pl.ds(half + quarter, quarter)

    k_next = {j: send(k_ref, kbuf.at[j, y], later(j)) for j in range(1, DOCUMENT_BLOCKS)}
    v_row = [send(v_ref, vbuf.at[0, y], at(0, 0, d)) for d in order]
    c_x = [send(w_ref.at[r, :, pc], wfull.at[z, x, y, r, :, pc], at(0, d, 0)) for d in order]
    k_row = [send(k_ref, kbuf.at[0, y], at(0, 0, d)) for d in order]
    z_order = (1, 7, 2, 6, 3, 5, 4)
    a_z = [send(w_ref.at[r, :, pa], wfull.at[z, x, y, r, :, pa], at(d, 0, 0)) for d in z_order]
    b_z = [send(w_ref.at[r, :, pb], wfull.at[z, x, y, r, :, pb], at(d, 0, 0)) for d in z_order]
    kbuf[0, y] = k_ref[...]
    vbuf[0, y] = v_ref[...]
    wfull[z, x, y, r] = w_ref[r]

    block = z * NX + x
    for j in range(1, DOCUMENT_BLOCKS):
        seen = (b_ref[block, jnp.maximum(block - j, 0)] == 1) & (block - j >= 0)
        bias[:, j * MASK_BLOCK_SIZE : (j + 1) * MASK_BLOCK_SIZE] = jnp.full(
            (tokens, MASK_BLOCK_SIZE), jnp.where(seen, 0.0, NEG), f32
        )
    for other in range(NY):
        rows = lax.broadcasted_iota(jnp.int32, (tokens, tokens), 0) + (y - other) * tokens
        cols = lax.broadcasted_iota(jnp.int32, (tokens, tokens), 1)
        bias[:, other * tokens : (other + 1) * tokens] = jnp.where(cols <= rows, 0.0, NEG)

    for j in range(1, DOCUMENT_BLOCKS):
        k_next[j].wait_recv()
        k_row += [send(kbuf.at[j, y], kbuf.at[j, y], at(0, 0, d)) for d in order]
    landed(v_row)
    v_next = [send(vbuf.at[0], vbuf.at[j], later(j)) for j in range(1, DOCUMENT_BLOCKS)]
    landed(c_x)
    c_y = [send(wfull.at[z, :, y, r, :, pc], wfull.at[z, :, y, r, :, pc], at(0, 0, d)) for d in order]
    landed(a_z)
    a_x = [send(wfull.at[:, x, y, r, :, pa], wfull.at[:, x, y, r, :, pa], at(0, d, 0)) for d in order]
    landed(b_z)
    b_y = [send(wfull.at[:, x, y, r, :, pb], wfull.at[:, x, y, r, :, pb], at(0, 0, d)) for d in order]
    landed(c_y)

    def ring(k, d):
        zz = lax.rem(z + (NZ - k if d == 0 else k), NZ)
        xs = pl.ds(0, NX) if k < 3 else pl.ds(2 * d, 2)
        piece = wfull.at[zz, xs, :, r, :, pc]
        return send(piece, piece, at(1 if d == 0 else NZ - 1, 0, 0))

    def share(piece):
        return send(piece, piece, partner)

    c_z = [ring(0, 0), ring(0, 1)]
    shared = [share(wfull.at[z, :, :, r, :, pc])]
    landed(a_x)
    a_y = [send(wfull.at[:, :, y, r, :, pa], wfull.at[:, :, y, r, :, pa], at(0, 0, d)) for d in order]
    landed(b_y)
    b_x = [send(wfull.at[:, x, :, r, :, pb], wfull.at[:, x, :, r, :, pb], at(0, d, 0)) for d in order]

    def forward(k):
        for d in range(2):
            c_z[d].wait_recv()
            if k < 4:
                c_z[d] = ring(k, d)
            zz = lax.rem(z + (NZ - k if d == 0 else k), NZ)
            xs = pl.ds(0, NX) if k < 4 else pl.ds(2 * d, 2)
            shared.append(share(wfull.at[zz, xs, :, r, :, pc]))

    landed(k_row)
    landed(v_next)

    factor = math.log2(math.e) / math.sqrt(HEAD_SIZE)
    keys_all = DOCUMENT_BLOCKS * MASK_BLOCK_SIZE

    def heads(hp, carry):
        first = pl.multiple_of(hp * 2 * HEAD_SIZE, 2 * HEAD_SIZE)
        group = pl.ds(pl.multiple_of((hp // 4) * HEAD_SIZE, HEAD_SIZE), HEAD_SIZE)
        one = pl.ds(first, HEAD_SIZE)
        two = pl.ds(first + HEAD_SIZE, HEAD_SIZE)
        both = jnp.concatenate([q_ref[:, one], q_ref[:, two]], axis=0)
        kk = kbuf[:, :, :, group].reshape(keys_all, HEAD_SIZE)
        s_ref[...] = lax.dot_general(both, kk, (((1,), (1,)), ((), ())), preferred_element_type=f32)

        def soft(i, inner):
            rows = pl.ds(pl.multiple_of(i * 16, 16), 16)
            v = s_ref[rows, :] + bias[pl.ds(pl.multiple_of(lax.rem(i, 8) * 16, 16), 16), :]
            m = jnp.max(v, axis=1, keepdims=True)
            e = jnp.exp2((v - m) * factor)
            l_ref[rows, :] = jnp.broadcast_to(jnp.sum(e, axis=1, keepdims=True), (16, HEAD_SIZE))
            p_ref[rows, :] = e.astype(bf16)
            return inner

        lax.fori_loop(0, 16, soft, 0)
        vv = vbuf[:, :, :, group].reshape(keys_all, HEAD_SIZE)
        o = jnp.dot(p_ref[...], vv, preferred_element_type=f32) / l_ref[...]
        att[:, one] = o[:tokens].astype(bf16)
        att[:, two] = o[tokens:].astype(bf16)
        return carry

    for k in range(1, 5):
        lax.fori_loop(2 * k - 2, 2 * k, heads, 0)
        forward(k)
    landed(a_y)
    shared.append(share(wfull.at[:, :, :, r, :, pa]))
    landed(b_x)
    shared.append(share(wfull.at[:, :, :, r, :, pb]))
    landed(shared)

    tile = 256

    def project(c, squares):
        cols = pl.ds(pl.multiple_of(c * tile, tile), tile)
        w = wfull[:, :, :, :, :, cols].reshape(width, tile)
        out = jnp.dot(att[...], w, preferred_element_type=f32) + r_ref[:, cols].astype(f32)
        out = out.astype(bf16)
        h_ref[:, cols] = out
        wide = out.astype(f32)
        return squares + jnp.sum(wide * wide, axis=1, keepdims=True)

    squares = lax.fori_loop(0, width // tile, project, jnp.zeros((tokens, 1), f32))
    scale = lax.rsqrt(squares / width + 1e-06)

    def norm(c, carry):
        cols = pl.ds(pl.multiple_of(c * tile, tile), tile)
        n_ref[:, cols] = (h_ref[:, cols].astype(f32) * scale * g_ref[:, cols]).astype(bf16)
        return carry

    lax.fori_loop(0, width // tile, norm, 0)
    for c in copies:
        c.wait_send()


def attention(queries, keys, values, residual, out_matrix, norm_gain, block_mask):
    rows, width = queries.shape
    bf16, f32 = jnp.bfloat16, jnp.float32
    vmem = pl.BlockSpec(memory_space=pltpu.VMEM)
    group = keys.shape[1]
    reach = DOCUMENT_BLOCKS * MASK_BLOCK_SIZE
    shape = jax.ShapeDtypeStruct((rows, width), bf16)
    return pl.pallas_call(
        attn_kernel,
        out_shape=(shape, shape),
        in_specs=[vmem] * 6 + [pl.BlockSpec(memory_space=pltpu.SMEM)],
        out_specs=(vmem, vmem),
        scratch_shapes=[
            pltpu.VMEM((DOCUMENT_BLOCKS, NY, rows, group), bf16),
            pltpu.VMEM((DOCUMENT_BLOCKS, NY, rows, group), bf16),
            pltpu.VMEM((NZ, NX, NY, 2, 8, width), bf16),
            pltpu.VMEM((rows, reach), f32),
            pltpu.VMEM((2 * rows, reach), f32),
            pltpu.VMEM((2 * rows, reach), bf16),
            pltpu.VMEM((2 * rows, HEAD_SIZE), f32),
            pltpu.VMEM((rows, width), bf16),
            pltpu.SemaphoreType.DMA((80,)),
            pltpu.SemaphoreType.DMA((80,)),
        ],
        compiler_params=pltpu.CompilerParams(collective_id=1, has_side_effects=True, vmem_limit_bytes=60 * 1024 * 1024),
        name="attn",
    )(queries, keys, values, residual, out_matrix.reshape(2, 8, width), norm_gain.reshape(1, width), block_mask)


def shards(
    queries,
    encoded_key_heads,
    value_head_vectors,
    residual,
    out_matrix,
    norm_gain,
    expert_ids,
    expert_gates,
    gate_matrix,
    lift_matrix,
    down_matrix,
    block_mask,
):
    normed, hidden_state = attention(
        queries, encoded_key_heads, value_head_vectors, residual, out_matrix, norm_gain, block_mask
    )
    meta = jnp.concatenate([expert_ids.astype(jnp.float32).T, expert_gates.T])
    return moe(normed, hidden_state, meta, gate_matrix, lift_matrix, down_matrix)


def solution(mesh):
    placed = (
        P(("rep", "ctx"), None),
        P(("rep", "ctx"), None),
        P(("rep", "ctx"), None),
        P(("rep", "ctx"), None),
        P("ctx", None),
        P(),
        P(("rep", "ctx"), None),
        P(("rep", "ctx"), None),
        P("ctx", None, None),
        P("ctx", None, None),
        P("ctx", None, None),
        P("rep", None),
    )
    return jax.shard_map(
        shards, mesh=mesh, in_specs=placed, out_specs=P(("rep", "ctx"), None), check_vma=False
    )
```

```python
import math

import jax
import jax.numpy as jnp
from jax import lax
from jax.experimental import pallas as pl
from jax.experimental.pallas import tpu as pltpu
from jax.sharding import PartitionSpec as P

QUERY_HEADS = 16
KEY_VALUE_HEADS = 2
HEAD_SIZE = 128
TOP = 8
MASK_BLOCK_SIZE = 512
DOCUMENT_BLOCKS = 4


MESH_ID = pl.DeviceIdType.MESH
PLANE = ((1, 0), (3, 0), (0, 1), (0, 3), (1, 1), (3, 3), (1, 3), (3, 1), (2, 0), (0, 2), (2, 1), (2, 3), (1, 2), (3, 2), (2, 2))
CAP = 9
NX, NY, NZ = 4, 4, 8
NQ = NX * NY
NEG = -1e30
COPIES = 112


def layer_kernel(
    q_ref,
    k_ref,
    v_ref,
    r_ref,
    w_ref,
    g_ref,
    b_ref,
    i_ref,
    t_ref,
    wg_hbm,
    wl_hbm,
    wd_hbm,
    o_ref,
    kbuf,
    vbuf,
    wfull,
    bias,
    s_ref,
    p_ref,
    l_ref,
    att,
    snd,
    rcv,
    h_ref,
    ids,
    gates,
    wg,
    wl,
    wd,
    xg,
    keys,
    gts,
    outbox,
    inbox,
    ret,
    xs,
    act,
    part,
    rsend,
    rrecv,
    w_sem,
    zs,
    zr,
    ds_,
    dr,
    bs,
    br,
    ss,
    sr,
):
    f32, bf16 = jnp.float32, jnp.bfloat16
    tokens, width = q_ref.shape
    me = lax.axis_index("ctx")
    r = lax.axis_index("rep")
    z = me // NQ
    q = lax.rem(me, NQ)
    x, y = q // NY, lax.rem(q, NY)
    total = NQ * NZ
    used = [0]

    def at(dz, dx, dy):
        return {"ctx": lax.rem(z + dz, NZ) * NQ + lax.rem(x + dx, NX) * NY + lax.rem(y + dy, NY)}

    def later(j):
        return {"ctx": lax.rem(me + j * NY, total)}

    def send(src, dst, dev):
        i = used[0]
        used[0] += 1
        c = pltpu.make_async_remote_copy(
            src_ref=src, dst_ref=dst, send_sem=snd.at[i], recv_sem=rcv.at[i], device_id=dev, device_id_type=MESH_ID
        )
        c.start()
        copies.append(c)
        return c

    weights = [
        pltpu.make_async_copy(a, b, w_sem.at[i])
        for i, (a, b) in enumerate(((wg_hbm.at[0], wg), (wl_hbm.at[0], wl), (wd_hbm.at[0], wd)))
    ]
    for c in weights:
        c.start()

    copies = []
    partner = {"rep": 1 - r}
    barrier = pltpu.get_barrier_semaphore()
    peers = [at(d, 0, 0) for d in range(1, NZ)] + [at(0, d, 0) for d in range(1, NX)] + [at(0, 0, d) for d in range(1, NY)]
    peers += [partner] + [later(j) for j in range(1, DOCUMENT_BLOCKS)]
    peers += [later(NQ * NZ // NY - j) for j in range(1, DOCUMENT_BLOCKS)]
    peers += [at(0, a, b) for a, b in PLANE]
    for dev in peers:
        pl.semaphore_signal(barrier, inc=1, device_id=dev, device_id_type=MESH_ID)
    pl.semaphore_wait(barrier, len(peers))

    def landed(cs):
        for c in cs:
            c.wait_recv()

    order = (1, 3, 2)
    z_order = (1, 7, 2, 6, 3, 5, 4)
    part_c, part_a = 3 * width // 8, 5 * width // 16
    pc, pa, pb = pl.ds(0, part_c), pl.ds(part_c, part_a), pl.ds(part_c + part_a, part_a)

    c_x = [send(w_ref.at[r, :, pc], wfull.at[z, x, y, r, :, pc], at(0, d, 0)) for d in order]
    k_next = {j: send(k_ref, kbuf.at[j, y], later(j)) for j in range(1, DOCUMENT_BLOCKS)}
    v_row = [send(v_ref, vbuf.at[0, y], at(0, 0, d)) for d in order]
    a_z = [send(w_ref.at[r, :, pa], wfull.at[z, x, y, r, :, pa], at(d, 0, 0)) for d in z_order]
    b_z = [send(w_ref.at[r, :, pb], wfull.at[z, x, y, r, :, pb], at(d, 0, 0)) for d in z_order]
    slot_of = {1: 1, 7: 2, 2: 3, 6: 4, 3: 5, 5: 6, 4: 7}
    tables = []
    for d in z_order:
        tables.append(send(i_ref, ids.at[slot_of[d]], at(d, 0, 0)))
        tables.append(send(t_ref, gates.at[slot_of[d]], at(d, 0, 0)))
    ids[0] = i_ref[...]
    gates[0] = t_ref[...]
    kbuf[0, y] = k_ref[...]
    vbuf[0, y] = v_ref[...]
    wfull[z, x, y, r] = w_ref[r]
    shared = []

    def share(piece):
        shared.append(send(piece, piece, partner))

    landed(c_x)
    c_y = [send(wfull.at[z, :, y, r, :, pc], wfull.at[z, :, y, r, :, pc], at(0, 0, d)) for d in order]
    k_row = [send(k_ref, kbuf.at[0, y], at(0, 0, d)) for d in order]
    for j in range(1, DOCUMENT_BLOCKS):
        k_next[j].wait_recv()
        k_row += [send(kbuf.at[j, y], kbuf.at[j, y], at(0, 0, d)) for d in order]
    landed(v_row)
    v_next = [send(vbuf.at[0], vbuf.at[j], later(j)) for j in range(1, DOCUMENT_BLOCKS)]

    def plane(k, d):
        return lax.rem(z + (NZ - k if d == 0 else k), NZ)

    def ring_parts(k):
        return [(d, e) for e in range(2) for d in range(2) if k < 3 or d == e]

    def ring_piece(k, d, e):
        return wfull.at[plane(k, d), pl.ds(2 * e, 2), :, r, :, pc]

    def ring(k, d, e):
        piece = ring_piece(k, d, e)
        return send(piece, piece, at(1 if d == 0 else NZ - 1, 0, 0))

    landed(c_y)
    c_z = {(d, e): ring(0, d, e) for d, e in ring_parts(0)}
    share(wfull.at[z, :, :, r, :, pc])

    def forward(k):
        for d, e in ring_parts(k - 1):
            c_z[d, e].wait_recv()
            if k < 4 and (d, e) in ring_parts(k):
                c_z[d, e] = ring(k, d, e)
            share(ring_piece(k, d, e))

    landed(a_z)
    a_x = [send(wfull.at[:, x, y, r, :, pa], wfull.at[:, x, y, r, :, pa], at(0, d, 0)) for d in order]
    landed(b_z)
    b_y = [send(wfull.at[:, x, y, r, :, pb], wfull.at[:, x, y, r, :, pb], at(0, 0, d)) for d in order]

    def last_a(i, zs):
        return wfull.at[zs, :, i, r, :, pa]

    def last_b(i, zs):
        return wfull.at[zs, i, :, r, :, pb]

    every = pl.ds(0, NZ)

    def step(of, i, d, zs):
        piece = of(i, zs)
        shift = 1 if d == 0 else NY - 1
        return send(piece, piece, at(0, 0, shift) if of is last_a else at(0, shift, 0))

    def begin(of, i):
        share(of(i, every))
        return [step(of, i, d, every) for d in range(2)]

    def pass_on(of, i, first):
        second = []
        for d in range(2):
            first[d].wait_recv()
            came = lax.rem(i + (NY - 1 if d == 0 else 1), NY)
            second.append(step(of, came, d, pl.ds(4 * d, 4)))
            share(of(came, every))
        return second

    def finish(of, i, second):
        for d in range(2):
            second[d].wait_recv()
            share(of(lax.rem(i + 2, NY), pl.ds(4 * d, 4)))

    block = z * NX + x
    for j in range(1, DOCUMENT_BLOCKS):
        seen = (b_ref[block, jnp.maximum(block - j, 0)] == 1) & (block - j >= 0)
        bias[:, j * MASK_BLOCK_SIZE : (j + 1) * MASK_BLOCK_SIZE] = jnp.full(
            (tokens, MASK_BLOCK_SIZE), jnp.where(seen, 0.0, NEG), f32
        )
    for other in range(NY):
        rows = lax.broadcasted_iota(jnp.int32, (tokens, tokens), 0) + (y - other) * tokens
        cols = lax.broadcasted_iota(jnp.int32, (tokens, tokens), 1)
        bias[:, other * tokens : (other + 1) * tokens] = jnp.where(cols <= rows, 0.0, NEG)


    landed(a_x)
    a_last = begin(last_a, y)
    landed(b_y)
    b_last = begin(last_b, x)
    forward(1)
    landed(tables)
    tri = (
        lax.broadcasted_iota(jnp.int32, (tokens, tokens), 0) < lax.broadcasted_iota(jnp.int32, (tokens, tokens), 1)
    ).astype(bf16)
    expert = (lax.broadcasted_iota(jnp.int32, (NQ, tokens), 0) + z * NQ)

    def block_keys(b):
        named, weight = ids[b], gates[b]
        chosen = jnp.zeros((NQ, tokens), f32)
        gate = jnp.zeros((NQ, tokens), f32)
        for k in range(TOP):
            hit = expert == named[k : k + 1, :]
            chosen = jnp.where(hit, 1.0, chosen)
            gate = jnp.where(hit, weight[k : k + 1, :], gate)
        rank = jnp.dot(chosen.astype(bf16), tri, preferred_element_type=f32)
        keys[b] = jnp.where(chosen > 0.5, rank, -100.0)
        gts[b] = gate

    def all_keys(b, carry):
        block_keys(b)
        return carry

    lax.fori_loop(0, NZ, all_keys, 0)
    landed(k_row)
    landed(v_next)
    forward(2)

    factor = math.log2(math.e) / math.sqrt(HEAD_SIZE)
    keys_all = DOCUMENT_BLOCKS * MASK_BLOCK_SIZE

    def heads(hp, carry):
        first = pl.multiple_of(hp * 2 * HEAD_SIZE, 2 * HEAD_SIZE)
        group = pl.ds(pl.multiple_of((hp // 4) * HEAD_SIZE, HEAD_SIZE), HEAD_SIZE)
        one = pl.ds(first, HEAD_SIZE)
        two = pl.ds(first + HEAD_SIZE, HEAD_SIZE)
        both = jnp.concatenate([q_ref[:, one], q_ref[:, two]], axis=0)
        kk = kbuf[:, :, :, group].reshape(keys_all, HEAD_SIZE)
        s_ref[...] = lax.dot_general(both, kk, (((1,), (1,)), ((), ())), preferred_element_type=f32)

        def soft(i, inner):
            rows = pl.ds(pl.multiple_of(i * 16, 16), 16)
            v = s_ref[rows, :] + bias[pl.ds(pl.multiple_of(lax.rem(i, 8) * 16, 16), 16), :]
            m = jnp.max(v, axis=1, keepdims=True)
            e = jnp.exp2((v - m) * factor)
            l_ref[rows, :] = jnp.broadcast_to(jnp.sum(e, axis=1, keepdims=True), (16, HEAD_SIZE))
            p_ref[rows, :] = e.astype(bf16)
            return inner

        lax.fori_loop(0, 16, soft, 0, unroll=8)
        vv = vbuf[:, :, :, group].reshape(keys_all, HEAD_SIZE)
        o = jnp.dot(p_ref[...], vv, preferred_element_type=f32) / l_ref[...]
        att[:, one] = o[:tokens].astype(bf16)
        att[:, two] = o[tokens:].astype(bf16)
        return carry

    lax.fori_loop(0, 2, heads, 0)
    a_end = pass_on(last_a, y, a_last)
    b_end = pass_on(last_b, x, b_last)
    forward(3)
    lax.fori_loop(2, 5, heads, 0)
    forward(4)
    finish(last_a, y, a_end)
    finish(last_b, x, b_end)
    lax.fori_loop(5, 8, heads, 0)
    landed(shared)

    tile = 256

    def project(c, squares):
        cols = pl.ds(pl.multiple_of(c * tile, tile), tile)
        w = wfull[:, :, :, :, :, cols].reshape(width, tile)
        out = jnp.dot(att[...], w, preferred_element_type=f32) + r_ref[:, cols].astype(f32)
        out = out.astype(bf16)
        h_ref[:, cols] = out
        wide = out.astype(f32)
        return squares + jnp.sum(wide * wide, axis=1, keepdims=True)

    squares = lax.fori_loop(0, width // tile, project, jnp.zeros((tokens, 1), f32))
    scale = lax.rsqrt(squares / width + 1e-06)

    def norm(c, carry):
        cols = pl.ds(pl.multiple_of(c * tile, tile), tile)
        xg[0, :, cols] = (h_ref[:, cols].astype(f32) * scale * g_ref[:, cols]).astype(bf16)
        return carry

    lax.fori_loop(0, width // tile, norm, 0)

    half = tokens // 2

    def zpeer(d):
        return lax.rem(z + d, NZ) * NQ + q

    def qpeer(i):
        return lax.rem(x + PLANE[i][0], NX) * NY + lax.rem(y + PLANE[i][1], NY)

    def remote(src, dst, s_sem, r_sem, dev):
        return pltpu.make_async_remote_copy(
            src_ref=src, dst_ref=dst, send_sem=s_sem, recv_sem=r_sem, device_id={"ctx": dev}, device_id_type=MESH_ID
        )

    def zcopy(d, k, h):
        src = xg.at[0] if k == 0 else xg.at[2 * k - 1 + d]
        rows = pl.ds(h * half, half)
        dst = xg.at[2 * k + 1 + d] if k < 3 else xg.at[7]
        return remote(src.at[rows], dst.at[rows], zs.at[d, k, h], zr.at[d, k, h], zpeer(1 if d == 0 else NZ - 1))

    def zparts(k):
        return [(d, h) for h in range(2) for d in range(2) if k < 3 or d == h]

    for d, h in zparts(0):
        zcopy(d, 0, h).start()
    row = lax.broadcasted_iota(jnp.int32, (NQ, 8, tokens), 1)

    def hits(b, first):
        return keys[b][:, None, :] == (row + first).astype(f32)

    def pick(b, first):
        return jnp.where(hits(b, first), 1.0, 0.0).reshape(NQ * 8, tokens).astype(bf16)

    def build(t, blocks):
        mats = [pick(b, first) for b, first in blocks]
        chunk = width // 4

        def piece(c, carry):
            cols = pl.ds(pl.multiple_of(c * chunk, chunk), chunk)
            total = None
            for (b, _), mat in zip(blocks, mats):
                one = jnp.dot(mat, xg[b, :, cols], preferred_element_type=f32)
                total = one if total is None else total + one
            outbox[t, :, :, cols] = total.astype(bf16).reshape(NQ, 8, chunk)
            return carry

        lax.fori_loop(0, 4, piece, 0)
        for i in range(NQ - 1):
            p = qpeer(i)
            remote(outbox.at[t, p], inbox.at[t, q], ds_.at[t], dr.at[t], z * NQ + p).start()
        inbox[t, q] = outbox[t, q]

    def dispatch(t):
        if isinstance(t, int) and t == 0:
            build(0, [(0, 0)])
        elif isinstance(t, int) and t == 8:
            build(8, [(7, 1)])
        else:
            build(t, [(t - 1, 9 - t), (t, -t)])

    def wait_all(buf, sem):
        pltpu.make_async_copy(buf, buf, sem).wait()

    def mlp(first, count):
        rows = count * NQ * 8

        def take(t, carry):
            wait_all(inbox.at[first + t, pl.ds(0, NQ - 1)], dr.at[first + t])
            xs[pl.ds(pl.multiple_of(t * NQ * 8, NQ * 8), NQ * 8), :] = inbox[first + t].reshape(NQ * 8, width)
            return carry

        lax.fori_loop(0, count, take, 0)
        hidden = wg.shape[1]
        tile = 256

        def up(c, carry):
            cols = pl.ds(pl.multiple_of(c * tile, tile), tile)
            g = jnp.dot(xs[pl.ds(0, rows), :], wg[:, cols], preferred_element_type=f32)
            u = jnp.dot(xs[pl.ds(0, rows), :], wl[:, cols], preferred_element_type=f32)
            act[pl.ds(0, rows), cols] = (g / (1.0 + jnp.exp(-g)) * u).astype(bf16)
            return carry

        lax.fori_loop(0, hidden // tile, up, 0)

        def down(c, carry):
            cols = pl.ds(pl.multiple_of(c * tile, tile), tile)
            y = jnp.dot(act[pl.ds(0, rows), :], wd[:, cols], preferred_element_type=f32)
            inbox[pl.ds(first, count), :, :, cols] = y.astype(bf16).reshape(count, NQ, 8, tile)
            return carry

        lax.fori_loop(0, width // tile, down, 0)

    def give_back(t):
        for i in range(NQ - 1):
            p = qpeer(i)
            remote(inbox.at[t, p], ret.at[t, q], bs.at[t], br.at[t], z * NQ + p).start()
        ret[t, q] = inbox[t, q]

    dispatch(0)
    groups = ((0, 3), (3, 2), (5, 2), (7, 2))
    for k in range(4):
        for d, h in zparts(k):
            zcopy(d, k, h).wait_recv()
            if k < 3 and (d, h) in zparts(k + 1):
                zcopy(d, k + 1, h).start()
        if k < 3:

            def two(t, carry):
                dispatch(t)
                return carry

            lax.fori_loop(2 * k + 1, 2 * k + 3, two, 0)
        else:
            dispatch(7)
            dispatch(8)
        if k == 0:
            for c in weights:
                c.wait()
        else:
            mlp(*groups[k - 1])
    mlp(*groups[3])

    def back(t, carry):
        give_back(8 - t)
        return carry

    lax.fori_loop(0, 9, back, 0)

    def wait_ret(t):
        wait_all(ret.at[t, pl.ds(0, NQ - 1)], br.at[t])

    def partial(b, slot):
        lo = jnp.where(hits(b, -b), gts[b][:, None, :], 0.0).reshape(NQ * 8, tokens)
        hi = jnp.where(hits(b, 8 - b), gts[b][:, None, :], 0.0).reshape(NQ * 8, tokens)
        mat = jnp.concatenate([lo, hi], axis=0).T.astype(bf16)
        chunk = width // 4

        def piece(c, carry):
            cols = pl.ds(pl.multiple_of(c * chunk, chunk), chunk)
            rows = ret[b : b + 2, :, :, cols].reshape(2 * NQ * 8, chunk)
            part[slot, :, cols] = jnp.dot(mat, rows, preferred_element_type=f32)
            return carry

        lax.fori_loop(0, 4, piece, 0)

    def scopy(d, k, h):
        rows = pl.ds(h * half, half)
        return remote(
            rsend.at[d, k, rows], rrecv.at[d, k, rows], ss.at[d, k, h], sr.at[d, k, h], zpeer(1 if d == 0 else NZ - 1)
        )

    def sparts(k):
        return [(d, h) for h in range(2) for d in range(2) if k > 0 or d == h]

    wait_ret(8)
    wait_ret(7)
    partial(7, 0)
    for d, h in sparts(0):
        rows = pl.ds(h * half, half)
        rsend[d, 0, rows] = part[0, rows].astype(bf16)
        scopy(d, 0, h).start()
    for k in range(1, 4):
        wait_ret(8 - 2 * k)
        wait_ret(7 - 2 * k)
        partial(8 - 2 * k, 0)
        partial(7 - 2 * k, 1)
        for d, h in sparts(k):
            rows = pl.ds(h * half, half)
            total = part[d, rows]
            if (d, h) in sparts(k - 1):
                scopy(d, k - 1, h).wait_recv()
                total = total + rrecv[d, k - 1, rows].astype(f32)
            rsend[d, k, rows] = total.astype(bf16)
            scopy(d, k, h).start()
    wait_ret(0)
    partial(0, 0)
    for h in range(2):
        rows = pl.ds(h * half, half)
        total = part[0, rows] + h_ref[rows, :].astype(f32)
        for d in range(2):
            scopy(d, 3, h).wait_recv()
            total = total + rrecv[d, 3, rows].astype(f32)
        o_ref[rows, :] = total.astype(bf16)

    for c in copies:
        c.wait_send()
    for k in range(4):
        for d, h in zparts(k):
            zcopy(d, k, h).wait_send()
        for d, h in sparts(k):
            scopy(d, k, h).wait_send()

    def sent(t, carry):
        wait_all(outbox.at[t, pl.ds(0, NQ - 1)], ds_.at[t])
        wait_all(inbox.at[t, pl.ds(0, NQ - 1)], bs.at[t])
        return carry

    lax.fori_loop(0, 9, sent, 0)


def layer(queries, keys, values, residual, out_matrix, norm_gain, block_mask, ids, gates, gate_matrix, lift_matrix, down_matrix):
    rows, width = queries.shape
    bf16, f32 = jnp.bfloat16, jnp.float32
    vmem = pl.BlockSpec(memory_space=pltpu.VMEM)
    hbm = pl.BlockSpec(memory_space=pl.ANY)
    dma = pltpu.SemaphoreType.DMA
    group, ff = keys.shape[1], gate_matrix.shape[2]
    reach = DOCUMENT_BLOCKS * MASK_BLOCK_SIZE
    return pl.pallas_call(
        layer_kernel,
        out_shape=jax.ShapeDtypeStruct((rows, width), bf16),
        in_specs=[vmem] * 6 + [pl.BlockSpec(memory_space=pltpu.SMEM), vmem, vmem, hbm, hbm, hbm],
        out_specs=vmem,
        scratch_shapes=[
            pltpu.VMEM((DOCUMENT_BLOCKS, NY, rows, group), bf16),
            pltpu.VMEM((DOCUMENT_BLOCKS, NY, rows, group), bf16),
            pltpu.VMEM((NZ, NX, NY, 2, 8, width), bf16),
            pltpu.VMEM((rows, reach), f32),
            pltpu.VMEM((2 * rows, reach), f32),
            pltpu.VMEM((2 * rows, reach), bf16),
            pltpu.VMEM((2 * rows, HEAD_SIZE), f32),
            pltpu.VMEM((rows, width), bf16),
            dma((COPIES,)),
            dma((COPIES,)),
            pltpu.VMEM((rows, width), bf16),
            pltpu.VMEM((NZ, TOP, rows), jnp.int32),
            pltpu.VMEM((NZ, TOP, rows), f32),
            pltpu.VMEM((width, ff), bf16),
            pltpu.VMEM((width, ff), bf16),
            pltpu.VMEM((ff, width), bf16),
            pltpu.VMEM((NZ, rows, width), bf16),
            pltpu.VMEM((NZ, NQ, rows), f32),
            pltpu.VMEM((NZ, NQ, rows), f32),
            pltpu.VMEM((CAP, NQ, 8, width), bf16),
            pltpu.VMEM((CAP, NQ, 8, width), bf16),
            pltpu.VMEM((CAP, NQ, 8, width), bf16),
            pltpu.VMEM((3 * NQ * 8, width), bf16),
            pltpu.VMEM((3 * NQ * 8, ff), bf16),
            pltpu.VMEM((2, rows, width), f32),
            pltpu.VMEM((2, 4, rows, width), bf16),
            pltpu.VMEM((2, 4, rows, width), bf16),
            dma((3,)),
            dma((2, 4, 2)),
            dma((2, 4, 2)),
            dma((CAP,)),
            dma((CAP,)),
            dma((CAP,)),
            dma((CAP,)),
            dma((2, 4, 2)),
            dma((2, 4, 2)),
        ],
        compiler_params=pltpu.CompilerParams(collective_id=0, has_side_effects=True, vmem_limit_bytes=61 * 1024 * 1024),
        name="layer",
    )(
        queries,
        keys,
        values,
        residual,
        out_matrix.reshape(2, 8, width),
        norm_gain.reshape(1, width),
        block_mask,
        ids,
        gates,
        gate_matrix,
        lift_matrix,
        down_matrix,
    )


def shards(
    queries,
    encoded_key_heads,
    value_head_vectors,
    residual,
    out_matrix,
    norm_gain,
    expert_ids,
    expert_gates,
    gate_matrix,
    lift_matrix,
    down_matrix,
    block_mask,
):
    return layer(
        queries,
        encoded_key_heads,
        value_head_vectors,
        residual,
        out_matrix,
        norm_gain,
        block_mask,
        expert_ids.T,
        expert_gates.T,
        gate_matrix,
        lift_matrix,
        down_matrix,
    )


def solution(mesh):
    placed = (
        P(("rep", "ctx"), None),
        P(("rep", "ctx"), None),
        P(("rep", "ctx"), None),
        P(("rep", "ctx"), None),
        P("ctx", None),
        P(),
        P(("rep", "ctx"), None),
        P(("rep", "ctx"), None),
        P("ctx", None, None),
        P("ctx", None, None),
        P("ctx", None, None),
        P("rep", None),
    )
    return jax.shard_map(
        shards, mesh=mesh, in_specs=placed, out_specs=P(("rep", "ctx"), None), check_vma=False
    )
```

```python
import math

import jax
import jax.numpy as jnp
from jax import lax
from jax.experimental import pallas as pl
from jax.experimental.pallas import tpu as pltpu
from jax.sharding import PartitionSpec as P

QUERY_HEADS = 16
KEY_VALUE_HEADS = 2
HEAD_SIZE = 128
TOP = 8
MASK_BLOCK_SIZE = 512
DOCUMENT_BLOCKS = 4


MESH_ID = pl.DeviceIdType.MESH
PLANE = ((1, 0), (3, 0), (0, 1), (0, 3), (1, 1), (3, 3), (1, 3), (3, 1), (2, 0), (0, 2), (2, 1), (2, 3), (1, 2), (3, 2), (2, 2))
CAP = 9
NX, NY, NZ = 4, 4, 8
NQ = NX * NY
NEG = -1e30
COPIES = 92


def layer_kernel(
    q_ref,
    k_ref,
    v_ref,
    r_ref,
    w_ref,
    g_ref,
    b_ref,
    i_ref,
    t_ref,
    wg_hbm,
    wl_hbm,
    wd_hbm,
    o_ref,
    kv,
    wfull,
    bias,
    s_ref,
    p_ref,
    l_ref,
    att,
    snd,
    rcv,
    h_ref,
    ids,
    gates,
    wg,
    wl,
    wd,
    xg,
    keys,
    gts,
    outbox,
    inbox,
    ret,
    xs,
    act,
    part,
    rsend,
    rrecv,
    w_sem,
    zs,
    zr,
    ds_,
    dr,
    bs,
    br,
    ss,
    sr,
):
    f32, bf16 = jnp.float32, jnp.bfloat16
    tokens, width = q_ref.shape
    me = lax.axis_index("ctx")
    r = lax.axis_index("rep")
    z = me // NQ
    q = lax.rem(me, NQ)
    x, y = q // NY, lax.rem(q, NY)
    total = NQ * NZ
    used = [0]

    def at(dz, dx, dy):
        return {"ctx": lax.rem(z + dz, NZ) * NQ + lax.rem(x + dx, NX) * NY + lax.rem(y + dy, NY)}

    def later(j):
        return {"ctx": lax.rem(me + j * NY, total)}

    def send(src, dst, dev):
        i = used[0]
        used[0] += 1
        c = pltpu.make_async_remote_copy(
            src_ref=src, dst_ref=dst, send_sem=snd.at[i], recv_sem=rcv.at[i], device_id=dev, device_id_type=MESH_ID
        )
        c.start()
        copies.append(c)
        return c

    weights = [
        pltpu.make_async_copy(a, b, w_sem.at[i])
        for i, (a, b) in enumerate(((wg_hbm.at[0], wg), (wl_hbm.at[0], wl), (wd_hbm.at[0], wd)))
    ]
    for c in weights:
        c.start()

    copies = []
    partner = {"rep": 1 - r}
    barrier = pltpu.get_barrier_semaphore()
    peers = [at(d, 0, 0) for d in range(1, NZ)] + [at(0, d, 0) for d in range(1, NX)] + [at(0, 0, d) for d in range(1, NY)]
    peers += [partner] + [later(j) for j in range(1, DOCUMENT_BLOCKS)]
    peers += [later(NQ * NZ // NY - j) for j in range(1, DOCUMENT_BLOCKS)]
    peers += [at(0, a, b) for a, b in PLANE]
    for dev in peers:
        pl.semaphore_signal(barrier, inc=1, device_id=dev, device_id_type=MESH_ID)
    pl.semaphore_wait(barrier, len(peers))

    def landed(cs):
        for c in cs:
            c.wait_recv()

    order = (1, 3, 2)
    z_order = (1, 7, 2, 6, 3, 5, 4)
    part_c = 7 * width // 16
    pc, pb = pl.ds(0, part_c), pl.ds(part_c, width - part_c)

    def along_y(src, dst, d):
        return send(src, dst, at(0, 0, 1 if d == 0 else NY - 1))

    c_x = [send(w_ref.at[r, :, pc], wfull.at[z, x, y, r, :, pc], at(0, d, 0)) for d in order]
    nexts = {
        j: [send(ref, kv.at[j, y, i], later(j)) for i, ref in enumerate((k_ref, v_ref))] for j in range(1, DOCUMENT_BLOCKS)
    }
    rows_of = {(0, d): [along_y(ref, kv.at[0, y, i], d) for i, ref in enumerate((k_ref, v_ref))] for d in range(2)}
    b_z = [send(w_ref.at[r, :, pb], wfull.at[z, x, y, r, :, pb], at(d, 0, 0)) for d in z_order]
    slot_of = {1: 1, 7: 2, 2: 3, 6: 4, 3: 5, 5: 6, 4: 7}
    tables = []
    for d in z_order:
        tables.append(send(i_ref, ids.at[slot_of[d]], at(d, 0, 0)))
        tables.append(send(t_ref, gates.at[slot_of[d]], at(d, 0, 0)))
    ids[0] = i_ref[...]
    gates[0] = t_ref[...]
    kv[0, y, 0] = k_ref[...]
    kv[0, y, 1] = v_ref[...]
    wfull[z, x, y, r] = w_ref[r]
    shared = []

    def share(piece):
        shared.append(send(piece, piece, partner))

    landed(c_x)
    c_y = [send(wfull.at[z, :, y, r, :, pc], wfull.at[z, :, y, r, :, pc], at(0, 0, d)) for d in order]
    for j in range(1, DOCUMENT_BLOCKS):
        landed(nexts[j])
        for d in range(2):
            rows_of[j, d] = [along_y(kv.at[j, y], kv.at[j, y], d)]
    relayed = []

    def relay(j):
        for d in range(2):
            landed(rows_of[j, d])
            came = lax.rem(y + (NY - 1 if d == 0 else 1), NY)
            relayed.append(along_y(kv.at[j, came, d], kv.at[j, came, d], d))

    def plane(k, d):
        return lax.rem(z + (NZ - k if d == 0 else k), NZ)

    def ring_parts(k):
        return [(d, e) for e in range(2) for d in range(2) if k < 3 or d == e]

    def ring_piece(k, d, e):
        return wfull.at[plane(k, d), pl.ds(2 * e, 2), :, r, :, pc]

    def ring(k, d, e):
        piece = ring_piece(k, d, e)
        return send(piece, piece, at(1 if d == 0 else NZ - 1, 0, 0))

    landed(c_y)
    c_z = {(d, e): ring(0, d, e) for d, e in ring_parts(0)}
    share(wfull.at[z, :, :, r, :, pc])

    def forward(k):
        for d, e in ring_parts(k - 1):
            c_z[d, e].wait_recv()
            if k < 4 and (d, e) in ring_parts(k):
                c_z[d, e] = ring(k, d, e)
            share(ring_piece(k, d, e))

    relay(0)
    landed(b_z)
    b_y = [send(wfull.at[:, x, y, r, :, pb], wfull.at[:, x, y, r, :, pb], at(0, 0, d)) for d in order]
    for j in range(1, DOCUMENT_BLOCKS):
        relay(j)

    def last_b(i, zs):
        return wfull.at[zs, i, :, r, :, pb]

    every = pl.ds(0, NZ)

    def step(of, i, d, zs):
        piece = of(i, zs)
        shift = 1 if d == 0 else NY - 1
        return send(piece, piece, at(0, shift, 0))

    def begin(of, i):
        share(of(i, every))
        return [step(of, i, d, every) for d in range(2)]

    def pass_on(of, i, first):
        second = []
        for d in range(2):
            first[d].wait_recv()
            came = lax.rem(i + (NY - 1 if d == 0 else 1), NY)
            second.append(step(of, came, d, pl.ds(4 * d, 4)))
            share(of(came, every))
        return second

    def finish(of, i, second):
        for d in range(2):
            second[d].wait_recv()
            share(of(lax.rem(i + 2, NY), pl.ds(4 * d, 4)))

    block = z * NX + x
    for j in range(1, DOCUMENT_BLOCKS):
        seen = (b_ref[block, jnp.maximum(block - j, 0)] == 1) & (block - j >= 0)
        bias[:, j * MASK_BLOCK_SIZE : (j + 1) * MASK_BLOCK_SIZE] = jnp.full(
            (tokens, MASK_BLOCK_SIZE), jnp.where(seen, 0.0, NEG), f32
        )
    for other in range(NY):
        rows = lax.broadcasted_iota(jnp.int32, (tokens, tokens), 0) + (y - other) * tokens
        cols = lax.broadcasted_iota(jnp.int32, (tokens, tokens), 1)
        bias[:, other * tokens : (other + 1) * tokens] = jnp.where(cols <= rows, 0.0, NEG)


    forward(1)
    landed(b_y)
    b_last = begin(last_b, x)
    landed(tables)
    tri = (
        lax.broadcasted_iota(jnp.int32, (tokens, tokens), 0) < lax.broadcasted_iota(jnp.int32, (tokens, tokens), 1)
    ).astype(bf16)
    expert = (lax.broadcasted_iota(jnp.int32, (NQ, tokens), 0) + z * NQ)

    def block_keys(b):
        named, weight = ids[b], gates[b]
        chosen = jnp.zeros((NQ, tokens), f32)
        gate = jnp.zeros((NQ, tokens), f32)
        for k in range(TOP):
            hit = expert == named[k : k + 1, :]
            chosen = jnp.where(hit, 1.0, chosen)
            gate = jnp.where(hit, weight[k : k + 1, :], gate)
        rank = jnp.dot(chosen.astype(bf16), tri, preferred_element_type=f32)
        keys[b] = jnp.where(chosen > 0.5, rank, -100.0)
        gts[b] = gate

    def all_keys(b, carry):
        block_keys(b)
        return carry

    lax.fori_loop(0, NZ, all_keys, 0)
    landed(relayed)
    forward(2)

    factor = math.log2(math.e) / math.sqrt(HEAD_SIZE)
    keys_all = DOCUMENT_BLOCKS * MASK_BLOCK_SIZE

    def heads(hp, carry):
        first = pl.multiple_of(hp * 2 * HEAD_SIZE, 2 * HEAD_SIZE)
        group = pl.ds(pl.multiple_of((hp // 4) * HEAD_SIZE, HEAD_SIZE), HEAD_SIZE)
        one = pl.ds(first, HEAD_SIZE)
        two = pl.ds(first + HEAD_SIZE, HEAD_SIZE)
        both = jnp.concatenate([q_ref[:, one], q_ref[:, two]], axis=0)
        kk = kv[:, :, 0, :, group].reshape(keys_all, HEAD_SIZE)
        s_ref[...] = lax.dot_general(both, kk, (((1,), (1,)), ((), ())), preferred_element_type=f32)

        def soft(i, inner):
            rows = pl.ds(pl.multiple_of(i * 16, 16), 16)
            v = s_ref[rows, :] + bias[pl.ds(pl.multiple_of(lax.rem(i, 8) * 16, 16), 16), :]
            m = jnp.max(v, axis=1, keepdims=True)
            e = jnp.exp2((v - m) * factor)
            l_ref[rows, :] = jnp.broadcast_to(jnp.sum(e, axis=1, keepdims=True), (16, HEAD_SIZE))
            p_ref[rows, :] = e.astype(bf16)
            return inner

        lax.fori_loop(0, 16, soft, 0, unroll=8)
        vv = kv[:, :, 1, :, group].reshape(keys_all, HEAD_SIZE)
        o = jnp.dot(p_ref[...], vv, preferred_element_type=f32) / l_ref[...]
        att[:, one] = o[:tokens].astype(bf16)
        att[:, two] = o[tokens:].astype(bf16)
        return carry

    lax.fori_loop(0, 2, heads, 0)
    b_end = pass_on(last_b, x, b_last)
    forward(3)
    lax.fori_loop(2, 5, heads, 0)
    forward(4)
    finish(last_b, x, b_end)
    lax.fori_loop(5, 8, heads, 0)
    landed(shared)

    tile = 256

    def project(c, squares):
        cols = pl.ds(pl.multiple_of(c * tile, tile), tile)
        w = wfull[:, :, :, :, :, cols].reshape(width, tile)
        out = jnp.dot(att[...], w, preferred_element_type=f32) + r_ref[:, cols].astype(f32)
        out = out.astype(bf16)
        h_ref[:, cols] = out
        wide = out.astype(f32)
        return squares + jnp.sum(wide * wide, axis=1, keepdims=True)

    squares = lax.fori_loop(0, width // tile, project, jnp.zeros((tokens, 1), f32))
    scale = lax.rsqrt(squares / width + 1e-06)

    def norm(c, carry):
        cols = pl.ds(pl.multiple_of(c * tile, tile), tile)
        xg[0, :, cols] = (h_ref[:, cols].astype(f32) * scale * g_ref[:, cols]).astype(bf16)
        return carry

    lax.fori_loop(0, width // tile, norm, 0)

    halves = [pl.ds(h * (width // 2), width // 2) for h in range(2)]
    others = pl.ds(0, NQ - 1)

    def zpeer(d):
        return lax.rem(z + d, NZ) * NQ + q

    def qpeer(i):
        a, b = PLANE[i]
        return lax.rem(x + a + (b - a + NX) * r, NX) * NY + lax.rem(y + b + (a - b + NX) * r, NY)

    def remote(src, dst, s_sem, r_sem, dev):
        return pltpu.make_async_remote_copy(
            src_ref=src, dst_ref=dst, send_sem=s_sem, recv_sem=r_sem, device_id={"ctx": dev}, device_id_type=MESH_ID
        )

    def zcopy(d, k, h):
        src = xg.at[0] if k == 0 else xg.at[2 * k - 1 + d]
        dst = xg.at[2 * k + 1 + d] if k < 3 else xg.at[7]
        cols = halves[h]
        return remote(src.at[:, cols], dst.at[:, cols], zs.at[d, k, h], zr.at[d, k, h], zpeer(1 if d == 0 else NZ - 1))

    def zparts(k):
        return [(d, h) for h in range(2) for d in range(2) if k < 3 or d == h]

    for d, h in zparts(0):
        zcopy(d, 0, h).start()
    row = lax.broadcasted_iota(jnp.int32, (NQ, 8, tokens), 1)
    chunk = width // 4

    def hits(b, first):
        return keys[b][:, None, :] == (row + first).astype(f32)

    def pick(b, first):
        return jnp.where(hits(b, first), 1.0, 0.0).reshape(NQ * 8, tokens).astype(bf16)

    def blocks_of(t):
        return [(b, 9 * (b == t - 1) - t) for b in (t - 1, t) if 0 <= b < NZ]

    def fill(t, mats, h):
        def piece(c, carry):
            cols = pl.ds(pl.multiple_of(c * chunk, chunk), chunk)
            total = None
            for (b, _), mat in zip(blocks_of(t), mats):
                one = jnp.dot(mat, xg[b, :, cols], preferred_element_type=f32)
                total = one if total is None else total + one
            outbox[t, :, :, cols] = total.astype(bf16).reshape(NQ, 8, chunk)
            return carry

        lax.fori_loop(2 * h, 2 * h + 2, piece, 0)

    def exchange(src, dst, tiles, cols, s_sem, r_sem):
        for i in range(NQ - 1):
            p = qpeer(i)
            remote(src.at[tiles, p, :, cols], dst.at[tiles, q, :, cols], s_sem, r_sem, z * NQ + p).start()
        dst[tiles, q, :, cols] = src[tiles, q, :, cols]

    def piece_of(k, h):
        return (pl.ds(0, 1), pl.ds(0, width), 0) if k < 0 else (pl.ds(2 * k + 1, 2), halves[h], 1 + 2 * k + h)

    def dispatch(k, h):
        tiles, cols, n = piece_of(k, h)
        exchange(outbox, inbox, tiles, cols, ds_.at[n], dr.at[n])

    def give_back(k, h):
        tiles, cols, n = piece_of(k, h)
        exchange(inbox, ret, tiles, cols, bs.at[n], br.at[n])

    def all_of(buf, sem, k, h):
        tiles, cols, n = piece_of(k, h)
        part_of = buf.at[tiles, others, :, cols]
        pltpu.make_async_copy(part_of, part_of, sem.at[n]).wait()

    pieces = [(-1, 0)] + [(k, h) for k in range(4) for h in range(2)]

    def mlp(first, count, finish_half):
        rows = pl.ds(0, count * NQ * 8)

        def take(t, carry):
            xs[pl.ds(pl.multiple_of(t * NQ * 8, NQ * 8), NQ * 8), :] = inbox[first + t].reshape(NQ * 8, width)
            return carry

        lax.fori_loop(0, count, take, 0)

        def up(c, carry):
            cols = pl.ds(pl.multiple_of(c * tile, tile), tile)
            g = jnp.dot(xs[rows, :], wg[:, cols], preferred_element_type=f32)
            u = jnp.dot(xs[rows, :], wl[:, cols], preferred_element_type=f32)
            act[rows, cols] = (g / (1.0 + jnp.exp(-g)) * u).astype(bf16)
            return carry

        lax.fori_loop(0, wg.shape[1] // tile, up, 0)

        def down(c, carry):
            cols = pl.ds(pl.multiple_of(c * tile, tile), tile)
            out = jnp.dot(act[rows, :], wd[:, cols], preferred_element_type=f32)
            inbox[pl.ds(first, count), :, :, cols] = out.astype(bf16).reshape(count, NQ, 8, tile)
            return carry

        steps = width // tile
        for h in range(2):
            lax.fori_loop(h * steps // 2, (h + 1) * steps // 2, down, 0)
            finish_half(h)

    for h in range(2):
        fill(0, [pick(*b) for b in blocks_of(0)], h)
    dispatch(-1, 0)
    for k in range(4):
        mats = [[pick(*b) for b in blocks_of(t)] for t in (2 * k + 1, 2 * k + 2)]
        for h in range(2):
            for d in range(2):
                if (d, h) in zparts(k):
                    zcopy(d, k, h).wait_recv()
                    if k < 3 and (d, h) in zparts(k + 1):
                        zcopy(d, k + 1, h).start()
            for t, mat in zip((2 * k + 1, 2 * k + 2), mats):
                fill(t, mat, h)
            dispatch(k, h)
        if k == 0:
            for c in weights:
                c.wait()
            all_of(inbox, dr, -1, 0)
        else:
            all_of(inbox, dr, k - 1, 0)
            all_of(inbox, dr, k - 1, 1)
            mlp(2 * k - 1 if k > 1 else 0, 2 if k > 1 else 3, lambda h: None)
    all_of(inbox, dr, 3, 0)
    all_of(inbox, dr, 3, 1)
    mlp(7, 2, lambda h: give_back(3, h))
    for k in (2, 1, 0):
        for h in range(2):
            give_back(k, h)
    give_back(-1, 0)

    def gated(b):
        lo = jnp.where(hits(b, -b), gts[b][:, None, :], 0.0).reshape(NQ * 8, tokens)
        hi = jnp.where(hits(b, 8 - b), gts[b][:, None, :], 0.0).reshape(NQ * 8, tokens)
        return jnp.concatenate([lo, hi], axis=0).T.astype(bf16)

    def partial(b, mat, slot, h):
        def piece(c, carry):
            cols = pl.ds(pl.multiple_of(c * chunk, chunk), chunk)
            rows = ret[b : b + 2, :, :, cols].reshape(2 * NQ * 8, chunk)
            part[slot, :, cols] = jnp.dot(mat, rows, preferred_element_type=f32)
            return carry

        lax.fori_loop(2 * h, 2 * h + 2, piece, 0)

    def scopy(d, k, h):
        cols = halves[h]
        return remote(
            rsend.at[d, k, :, cols],
            rrecv.at[d, k, :, cols],
            ss.at[d, k, h],
            sr.at[d, k, h],
            zpeer(1 if d == 0 else NZ - 1),
        )

    def sparts(k):
        return [(d, h) for h in range(2) for d in range(2) if k > 0 or d == h]

    mat = gated(7)
    for h in range(2):
        cols = halves[h]
        all_of(ret, br, 3, h)
        partial(7, mat, 0, h)
        rsend[h, 0, :, cols] = part[0, :, cols].astype(bf16)
        scopy(h, 0, h).start()
    for k in range(1, 4):
        mats = [gated(8 - 2 * k), gated(7 - 2 * k)]
        for h in range(2):
            cols = halves[h]
            all_of(ret, br, 3 - k, h)
            for d in range(2):
                partial(8 - 2 * k - d, mats[d], d, h)
            for d in range(2):
                total = part[d, :, cols]
                if (d, h) in sparts(k - 1):
                    scopy(d, k - 1, h).wait_recv()
                    total = total + rrecv[d, k - 1, :, cols].astype(f32)
                rsend[d, k, :, cols] = total.astype(bf16)
                scopy(d, k, h).start()
    mat = gated(0)
    all_of(ret, br, -1, 0)
    for h in range(2):
        cols = halves[h]
        partial(0, mat, 0, h)
        total = part[0, :, cols] + h_ref[:, cols].astype(f32)
        for d in range(2):
            scopy(d, 3, h).wait_recv()
            total = total + rrecv[d, 3, :, cols].astype(f32)
        o_ref[:, cols] = total.astype(bf16)

    for c in copies:
        c.wait_send()
    for k in range(4):
        for d, h in zparts(k):
            zcopy(d, k, h).wait_send()
        for d, h in sparts(k):
            scopy(d, k, h).wait_send()
    for k, h in pieces:
        all_of(outbox, ds_, k, h)
        all_of(inbox, bs, k, h)


def layer(queries, keys, values, residual, out_matrix, norm_gain, block_mask, ids, gates, gate_matrix, lift_matrix, down_matrix):
    rows, width = queries.shape
    bf16, f32 = jnp.bfloat16, jnp.float32
    vmem = pl.BlockSpec(memory_space=pltpu.VMEM)
    hbm = pl.BlockSpec(memory_space=pl.ANY)
    dma = pltpu.SemaphoreType.DMA
    group, ff = keys.shape[1], gate_matrix.shape[2]
    reach = DOCUMENT_BLOCKS * MASK_BLOCK_SIZE
    return pl.pallas_call(
        layer_kernel,
        out_shape=jax.ShapeDtypeStruct((rows, width), bf16),
        in_specs=[vmem] * 6 + [pl.BlockSpec(memory_space=pltpu.SMEM), vmem, vmem, hbm, hbm, hbm],
        out_specs=vmem,
        scratch_shapes=[
            pltpu.VMEM((DOCUMENT_BLOCKS, NY, 2, rows, group), bf16),
            pltpu.VMEM((NZ, NX, NY, 2, 8, width), bf16),
            pltpu.VMEM((rows, reach), f32),
            pltpu.VMEM((2 * rows, reach), f32),
            pltpu.VMEM((2 * rows, reach), bf16),
            pltpu.VMEM((2 * rows, HEAD_SIZE), f32),
            pltpu.VMEM((rows, width), bf16),
            dma((COPIES,)),
            dma((COPIES,)),
            pltpu.VMEM((rows, width), bf16),
            pltpu.VMEM((NZ, TOP, rows), jnp.int32),
            pltpu.VMEM((NZ, TOP, rows), f32),
            pltpu.VMEM((width, ff), bf16),
            pltpu.VMEM((width, ff), bf16),
            pltpu.VMEM((ff, width), bf16),
            pltpu.VMEM((NZ, rows, width), bf16),
            pltpu.VMEM((NZ, NQ, rows), f32),
            pltpu.VMEM((NZ, NQ, rows), f32),
            pltpu.VMEM((CAP, NQ, 8, width), bf16),
            pltpu.VMEM((CAP, NQ, 8, width), bf16),
            pltpu.VMEM((CAP, NQ, 8, width), bf16),
            pltpu.VMEM((3 * NQ * 8, width), bf16),
            pltpu.VMEM((3 * NQ * 8, ff), bf16),
            pltpu.VMEM((2, rows, width), f32),
            pltpu.VMEM((2, 4, rows, width), bf16),
            pltpu.VMEM((2, 4, rows, width), bf16),
            dma((3,)),
            dma((2, 4, 2)),
            dma((2, 4, 2)),
            dma((CAP,)),
            dma((CAP,)),
            dma((CAP,)),
            dma((CAP,)),
            dma((2, 4, 2)),
            dma((2, 4, 2)),
        ],
        compiler_params=pltpu.CompilerParams(collective_id=0, has_side_effects=True, vmem_limit_bytes=61 * 1024 * 1024),
        name="layer",
    )(
        queries,
        keys,
        values,
        residual,
        out_matrix.reshape(2, 8, width),
        norm_gain.reshape(1, width),
        block_mask,
        ids,
        gates,
        gate_matrix,
        lift_matrix,
        down_matrix,
    )


def shards(
    queries,
    encoded_key_heads,
    value_head_vectors,
    residual,
    out_matrix,
    norm_gain,
    expert_ids,
    expert_gates,
    gate_matrix,
    lift_matrix,
    down_matrix,
    block_mask,
):
    return layer(
        queries,
        encoded_key_heads,
        value_head_vectors,
        residual,
        out_matrix,
        norm_gain,
        block_mask,
        expert_ids.T,
        expert_gates.T,
        gate_matrix,
        lift_matrix,
        down_matrix,
    )


def solution(mesh):
    placed = (
        P(("rep", "ctx"), None),
        P(("rep", "ctx"), None),
        P(("rep", "ctx"), None),
        P(("rep", "ctx"), None),
        P("ctx", None),
        P(),
        P(("rep", "ctx"), None),
        P(("rep", "ctx"), None),
        P("ctx", None, None),
        P("ctx", None, None),
        P("ctx", None, None),
        P("rep", None),
    )
    return jax.shard_map(
        shards, mesh=mesh, in_specs=placed, out_specs=P(("rep", "ctx"), None), check_vma=False
    )
```
